512 devices in a mesh: seq: 128 (over x, z, core), head: 4 (over y).
Axes of the slice: x: 4, y: 4, z: 16, core: 2. Of those that a mesh axis runs over, the one named last changes fastest.
Arguments:
- queries: bfloat16 [65536, 2048], P('seq', 'head'), may hold values from -6 to 6
- keys: bfloat16 [65536, 2048], P('seq', 'head'), may hold values from -6 to 6
- values: bfloat16 [65536, 2048], P('seq', 'head'), may hold values from -6 to 6
- summary_lists: int32 [128, 8, 16], P('seq', 'head'), may hold values from 0 to 126, as said below
- out_weight: bfloat16 [2048, 2048], P('head'), may hold values from -0.125 to 0.125
Outputs:
- mixed: bfloat16 [65536, 2048], P(('seq', 'head'))
The draws below stay inside these ranges and needn't reach their ends.
Inputs may be any that keep to these rules, and one draw needn't show every extreme that they name: `summary_lists`: entry [b, f, k] names a block. In every query block b above 0 it is below b, and entry [b, f, 0] is b - 1; in query block 0 every entry is 0 and names nothing. Entries may repeat.
All inputs are finite; a program needn't handle non-finite values.
Results may differ from the reference program's by a relative error of at most 0.014.
Values may be sent and summed in bfloat16 or wider, within the bound.
A program may use at most 64 MiB of HBM per device.

```python
import jax
import jax.numpy as jnp
from jax import lax

HEADS = 16
HEAD_DIM = 128
BLK = 512
SUMMARY = 32
PICKS = 16
D = 2048
NBLK = 128
TOKENS = 65536


def draw_queries(key, part):
    noise_key = jax.random.fold_in(key, 11)
    field = jnp.clip(1.2 * jax.random.normal(noise_key, (TOKENS, D), jnp.float32), -6.0, 6.0)
    return field.astype(jnp.bfloat16)


def draw_keys(key, part):
    noise_key = jax.random.fold_in(key, 13)
    field = jnp.clip(1.2 * jax.random.normal(noise_key, (TOKENS, D), jnp.float32), -6.0, 6.0)
    return field.astype(jnp.bfloat16)


def draw_summary_lists(key, part):
    block = jnp.arange(NBLK, dtype=jnp.int32)[:, None, None]
    upper = jnp.maximum(block, 1)
    picked = jax.random.randint(key, (NBLK, HEADS // 2, PICKS), 0, upper, dtype=jnp.int32)
    before = jnp.broadcast_to(jnp.maximum(block - 1, 0), (NBLK, HEADS // 2, 1))
    return jnp.concatenate([before, picked[:, :, 1:]], axis=2).astype(jnp.int32)


def block_scale(own_key, dims, cuts, least, top_value):
    level = 1.0
    for axis_at, parts in cuts:
        draws = jax.random.uniform(jax.random.fold_in(jax.random.fold_in(own_key, 6), axis_at), (parts,), jnp.float32, least / len(cuts), top_value / len(cuts))
        level = level * jnp.repeat(jnp.exp(draws), dims[axis_at] // parts).reshape((-1,) + (1,) * (len(dims) - 1 - axis_at))
    return level


def gaussian(stream_key, extent, width, bound, cuts=(), kind=jnp.bfloat16):
    values = width * jax.random.normal(stream_key, extent, jnp.float32)
    if cuts:
        values = values * block_scale(stream_key, extent, cuts, -0.22, 0.18)
    return jnp.clip(values, -bound, bound).astype(kind)


def setup_inputs(seed: int = 0) -> dict:
    arg_keys = jax.random.split(jax.random.key(seed), 6)
    queries = draw_queries(jax.random.fold_in(arg_keys[5], 71), 0)
    keys = draw_keys(jax.random.fold_in(arg_keys[5], 71), 0)
    values = gaussian(arg_keys[2], (TOKENS, D), 1.5, 6.0, ((0, 128), (1, 4)))
    summary_lists = draw_summary_lists(jax.random.fold_in(arg_keys[5], 71), 0)
    out_weight = gaussian(arg_keys[4], (D, D), D ** -0.5, 0.125, ((0, 4),))
    return {"queries": queries, "keys": keys, "values": values, "summary_lists": summary_lists, "out_weight": out_weight}


NEG = -1e30


def masked_softmax(scores, valid):
    scores = jnp.where(valid, scores, NEG)
    peak = jnp.max(scores, axis=-1, keepdims=True)
    weights = jnp.where(valid, jnp.exp(scores - peak), 0.0)
    return weights / jnp.sum(weights, axis=-1, keepdims=True)


def row_head(head_q, head_k, head_v):
    scale = HEAD_DIM ** -0.5
    causal = jnp.arange(BLK)[:, None] >= jnp.arange(BLK)[None, :]

    def one_block(block):
        block_q, block_k, block_v = block
        scores = jnp.dot(block_q, block_k.T, preferred_element_type=jnp.float32) * scale
        weights = masked_softmax(scores, causal).astype(jnp.bfloat16)
        return jnp.dot(weights, block_v, preferred_element_type=jnp.float32).astype(jnp.bfloat16)

    return lax.map(one_block, (head_q, head_k, head_v))


def column_head(head_q, head_k, head_v):
    scale = HEAD_DIM ** -0.5
    col_q = jnp.swapaxes(head_q, 0, 1).astype(jnp.float32)
    col_k = jnp.swapaxes(head_k, 0, 1).astype(jnp.float32)
    col_v = jnp.swapaxes(head_v, 0, 1).astype(jnp.float32)
    scores = jnp.einsum('crd,csd->crs', col_q, col_k) * scale
    earlier = jnp.arange(NBLK)[:, None] >= jnp.arange(NBLK)[None, :]
    weights = masked_softmax(scores, earlier[None]).astype(jnp.bfloat16)
    result = jnp.einsum('crs,csd->crd', weights.astype(jnp.float32), col_v)
    return jnp.swapaxes(result, 0, 1).astype(jnp.bfloat16)


def fixed_head(head_q, head_k, head_v, lists):
    scale = HEAD_DIM ** -0.5
    causal = jnp.arange(BLK)[:, None] >= jnp.arange(BLK)[None, :]
    tail_k = head_k[:, BLK - SUMMARY:, :]
    tail_v = head_v[:, BLK - SUMMARY:, :]

    def one_block(item):
        block_q, block_k, block_v, picks, index = item
        own_scores = jnp.dot(block_q, block_k.T, preferred_element_type=jnp.float32) * scale
        far_k = tail_k[picks].reshape(PICKS * SUMMARY, HEAD_DIM)
        far_v = tail_v[picks].reshape(PICKS * SUMMARY, HEAD_DIM)
        far_scores = jnp.dot(block_q, far_k.T, preferred_element_type=jnp.float32) * scale
        usable = jnp.repeat(picks < index, SUMMARY)
        scores = jnp.concatenate([own_scores, far_scores], axis=1)
        valid = jnp.concatenate([causal, jnp.broadcast_to(usable[None, :], (BLK, PICKS * SUMMARY))], axis=1)
        weights = masked_softmax(scores, valid).astype(jnp.bfloat16)
        stacked = jnp.concatenate([block_v, far_v], axis=0)
        return jnp.dot(weights, stacked, preferred_element_type=jnp.float32).astype(jnp.bfloat16)

    return lax.map(one_block, (head_q, head_k, head_v, lists, jnp.arange(NBLK, dtype=jnp.int32)))


def reference(queries, keys, values, summary_lists, out_weight):
    def head_part(source, head):
        return source[:, head * HEAD_DIM:(head + 1) * HEAD_DIM].reshape(NBLK, BLK, HEAD_DIM)

    pieces = []
    for head in range(HEADS):
        head_q = head_part(queries, head)
        head_k = head_part(keys, head)
        head_v = head_part(values, head)
        kind = head % 4
        if kind == 0:
            result = row_head(head_q, head_k, head_v)
        elif kind == 1:
            result = column_head(head_q, head_k, head_v)
        else:
            result = fixed_head(head_q, head_k, head_v, summary_lists[:, 2 * (head // 4) + kind - 2, :])
        pieces.append(result.reshape(TOKENS, HEAD_DIM))
    attended = jnp.concatenate(pieces, axis=1)
    return jnp.dot(attended, out_weight, preferred_element_type=jnp.float32).astype(jnp.bfloat16)
```

```python
import functools
import math

import jax
import jax.numpy as jnp
from jax import lax
from jax.experimental import pallas as pl
from jax.experimental.pallas import tpu as pltpu
from jax.sharding import PartitionSpec as P

MESH = pl.DeviceIdType.MESH
HD = 128
BLK = 512
NX, NZ, NC, NY = 4, 16, 2, 4
PICKS = 16
SUM = 32
NEG = -1e30
EXPC = (HD ** -0.5) * math.log2(math.e)
QC = 256
OC = 0
BF = jnp.bfloat16
F32 = jnp.float32


def dot_t(a, b):
    return lax.dot_general(a, b, (((1,), (1,)), ((), ())), preferred_element_type=F32)


def dot(a, b):
    return jnp.dot(a, b, preferred_element_type=F32)


def kernel(
    lists, q, k, v, q3, k3, v3, k2, v2, w,
    out,
    tiles, wbuf, abuf, stage, c1, c2, obuf, r1, colout, orow, ofix,
    cf, cfo, acc_s, m_s, l_s, fark, farv, pbuf, prcv,
    lsem, wlsem, wssem, wrsem, tsend, zl, zr, xl, xr, x2sem, psem,
    a2s, a2r, p2s, p2r, r1s, r1r, r2s, r2r, ysend, asem, fsend, frecv,
):
    seq = lax.axis_index("seq")
    y = lax.axis_index("head")
    x = seq // (NZ * NC)
    z = (seq // NC) % NZ
    c = seq % NC
    oth = 1 - c

    def dev(xx, zz, cc, yy):
        return ((xx * NZ + zz) * NC + cc, yy)

    def rcopy(src, dst, ss, rs, to):
        return pltpu.make_async_remote_copy(
            src_ref=src, dst_ref=dst, send_sem=ss, recv_sem=rs, device_id=to, device_id_type=MESH
        )

    def wait_bytes(ref, sem):
        pltpu.make_async_copy(ref, ref, sem).wait()

    bar = pltpu.get_barrier_semaphore()

    def greet(to):
        pl.semaphore_signal(bar, inc=1, device_id=to, device_id_type=MESH)

    def greet_z(i, carry):
        greet(dev(x, (z + i) % NZ, c, y))
        return carry

    lax.fori_loop(1, NZ, greet_z, 0)
    for dx in range(NX):
        for dc in range(NC):
            if dx or dc:
                greet(dev((x + dx) % NX, z, (c + dc) % NC, y))
    for dy in range(1, NY):
        for dc in range(NC):
            greet(dev(x, z, (c + dc) % NC, (y + dy) % NY))

    own = c * 64 + x * NZ + z
    local = []
    for t, src in enumerate((q3, k3, v3)):
        local.append(pltpu.make_async_copy(src.at[:, :, HD : 2 * HD], stage.at[t], lsem.at[t]))
    for f in range(2):
        for t, src in enumerate((k2, v2)):
            local.append(
                pltpu.make_async_copy(
                    src.at[BLK - SUM : BLK, (2 + f) * HD : (3 + f) * HD],
                    tiles.at[own, f, t],
                    lsem.at[3 + 2 * f + t],
                )
            )
    for h in range(2):
        local.append(
            pltpu.make_async_copy(
                w.at[pl.ds(pl.multiple_of((2 * h + c) * HD, HD), HD)],
                wbuf.at[pl.ds(pl.multiple_of((y * 2 + h) * HD, HD), HD)],
                wlsem.at[h],
            )
        )
    for cp in local:
        cp.start()

    def own_attention(head, i):
        qi = q[i * QC : (i + 1) * QC, head * HD : (head + 1) * HD]
        n = (i + 1) * QC
        s = dot_t(qi, k[:n, head * HD : (head + 1) * HD])
        rows = lax.broadcasted_iota(jnp.int32, (QC, n), 0) + i * QC
        cols = lax.broadcasted_iota(jnp.int32, (QC, n), 1)
        s = jnp.where(rows >= cols, s, NEG)
        m = jnp.max(s, axis=1, keepdims=True)
        p = jnp.exp2((s - m) * EXPC)
        l = jnp.sum(p, axis=1, keepdims=True)
        acc = dot(p.astype(BF), v[:n, head * HD : (head + 1) * HD])
        return m, l, acc

    for i in range(BLK // QC):
        m, l, acc = own_attention(0, i)
        orow[i * (QC // 8) : (i + 1) * (QC // 8)] = (acc / l).astype(BF).reshape(QC // 8, 8, HD)
    for f in range(2):
        for i in range(BLK // QC):
            m, l, acc = own_attention(2 + f, i)
            rs = slice(i * QC, (i + 1) * QC)
            acc_s[f, rs, :] = acc
            m_s[f, rs, :] = jnp.broadcast_to(m, (QC, HD))
            l_s[f, rs, :] = jnp.broadcast_to(l, (QC, HD))

    for cp in local:
        cp.wait()
    pl.semaphore_wait(bar, (NZ - 1) + (NX * NC - 1) + (NY - 1) * NC)

    def wrows(yy, h):
        return wbuf.at[pl.ds(pl.multiple_of((yy * 2 + h) * HD, HD), HD)]

    yr, yl, y2 = (y + 1) % NY, (y + NY - 1) % NY, (y + 2) % NY
    wsends = []

    def wsend(n, yy, h, to, rsem):
        cp = rcopy(wrows(yy, h), wrows(yy, h), wssem.at[n], rsem, dev(x, z, c, to))
        cp.start()
        wsends.append(cp)

    def wsend_first():
        wsend(0, y, 0, yr, wrsem.at[0])
        wsend(1, y, 1, yl, wrsem.at[3])
        wsend(2, y, 1, yr, wrsem.at[1])
        wsend(3, y, 0, yl, wrsem.at[2])

    def wrelay():
        wait_bytes(wrows(yl, 0), wrsem.at[0])
        wsend(4, yl, 0, yr, wrsem.at[4])
        wait_bytes(wrows(yr, 1), wrsem.at[3])
        wsend(5, yr, 1, yl, wrsem.at[5])

    ysends = []

    def attended_send(n, src_of, tc, h):
        lanes = pl.ds(pl.multiple_of((y * 2 + h) * HD, HD), HD)
        dst = abuf.at[c, :, :, lanes]
        for dy in range(1, NY):
            yy = (y + dy) % NY
            cp = rcopy(src_of(yy), dst, ysend.at[n, dy], asem, dev(x, z, tc, yy))
            cp.start()
            ysends.append((cp, None))
        near = rcopy(src_of(y), dst, ysend.at[n, 0], asem, dev(x, z, oth, y))
        ysends.append((near, tc))

        @pl.when(c == tc)
        def _():
            pltpu.make_async_copy(src_of(y), dst, asem).start()

        @pl.when(c != tc)
        def _():
            near.start()

    def quarter(ref):
        return lambda yy: ref.at[pl.ds(pl.multiple_of(yy * 16, 16), 16)]

    xr_, xl_, x2_ = (x + 1) % NX, (x + NX - 1) % NX, (x + 2) % NX

    def slot(xx, zz):
        return c * 64 + xx * NZ + zz

    def zm(d):
        return (z + d + NZ) % NZ

    def tsend_to(src, rs, to):
        rcopy(src, src, tsend, rs, to).start()

    def ring_send(s):
        right, left = dev(x, zm(1), c, y), dev(x, zm(-1), c, y)
        if s < 8:
            tsend_to(tiles.at[slot(x, zm(1 - s))], zl.at[s], right)
            tsend_to(tiles.at[slot(x, zm(s - 1))], zr.at[s], left)
        else:
            tsend_to(tiles.at[slot(x, zm(-7)), 0], zl.at[8], right)
            tsend_to(tiles.at[slot(x, zm(7)), 1], zr.at[8], left)

    def ring_wait(s):
        if s < 8:
            wait_bytes(tiles.at[slot(x, zm(-s))], zl.at[s])
            wait_bytes(tiles.at[slot(x, zm(s))], zr.at[s])
        else:
            wait_bytes(tiles.at[slot(x, zm(8)), 0], zl.at[8])
            wait_bytes(tiles.at[slot(x, zm(8)), 1], zr.at[8])

    def members(n):
        if n == 0:
            return [z]
        if n == 8:
            return [zm(8)]
        return [zm(-n), zm(n)]

    partner = dev(x, z, oth, y)

    def forward(n):
        for zz in members(n):
            src = tiles.at[slot(x, zz)]
            tsend_to(src, xl.at[zz], dev(xr_, z, c, y))
            tsend_to(src, xr.at[zz], dev(xl_, z, c, y))
            tsend_to(src, psem, partner)

    def relay(n):
        for zz in members(n):
            src = tiles.at[slot(xl_, zz)]
            wait_bytes(src, xl.at[zz])
            tsend_to(src.at[0], x2sem.at[0], dev(xr_, z, c, y))
            tsend_to(src, psem, partner)
            src = tiles.at[slot(xr_, zz)]
            wait_bytes(src, xr.at[zz])
            tsend_to(src.at[1], x2sem.at[1], dev(xl_, z, c, y))
            tsend_to(src, psem, partner)

    def col_send(d):
        zz = zm(d)
        rcopy(
            stage.at[:, pl.ds(zz * 4, 4)], c1.at[z], a2s, a2r.at[z], dev(x, zz, c, y)
        ).start()

    own_piece = pltpu.make_async_copy(stage.at[:, pl.ds(z * 4, 4)], c1.at[z], lsem.at[7])
    own_piece.start()

    wsend_first()
    for s in range(1, 9):
        ring_send(s)
        if s == 1:
            col_send(8)
        else:
            col_send(9 - s)
            col_send(s - 9)
        forward(s - 1)
        if s >= 2:
            relay(s - 2)
        if s == 2:
            attended_send(0, quarter(orow), 0, 0)
        if s == 6:
            wrelay()
        ring_wait(s)
    forward(8)

    own_piece.wait()
    for d in range(1, NZ):
        zz = zm(d)
        wait_bytes(c1.at[zz], a2r.at[zz])
    src_id = x * NC + c
    p2 = []
    for dx in range(NX):
        g = (x + dx) % NX
        p2.append(rcopy(c1.at[:, :, g], c2.at[src_id], p2s.at[dx], p2r, dev(g, z, OC, y)))
    for dx in range(1, NX):
        p2[dx].start()

    @pl.when(c == OC)
    def _():
        pltpu.make_async_copy(c1.at[:, :, x], c2.at[src_id], p2r).start()

    @pl.when(c != OC)
    def _():
        p2[0].start()

    relay(7)
    relay(8)
    far2 = tiles.at[pl.ds(slot(x2_, 0), NZ)]
    wait_bytes(far2.at[:, 0], x2sem.at[0])
    wait_bytes(far2.at[:, 1], x2sem.at[1])
    tsend_to(far2, psem, partner)

    @pl.when(c == OC)
    def _():
        wait_bytes(c2, p2r)
        for t in range(3):
            cf[t] = c2[:, :, t].astype(F32).reshape(NBLK8, HD)

        def blk(r):
            return (r // 32) * 32 + (r % 16) * 2 + (r // 16) % 2

        rq = blk(lax.broadcasted_iota(jnp.int32, (128, 128), 0))
        rk = blk(lax.broadcasted_iota(jnp.int32, (128, 128), 1))
        ok = rq >= rk
        for j in range(8):
            cols = pl.ds(j, 128, stride=8)
            qc = cf[0, cols, :].astype(BF)
            kc = cf[1, cols, :].astype(BF)
            vc = cf[2, cols, :].astype(BF)
            s = jnp.where(ok, dot_t(qc, kc), NEG)
            m = jnp.max(s, axis=1, keepdims=True)
            p = jnp.exp2((s - m) * EXPC)
            l = jnp.sum(p, axis=1, keepdims=True)
            cfo[cols, :] = dot(p.astype(BF), vc) / l
        obuf[...] = cfo[...].astype(BF).reshape(NX * NC, NZ, 8, HD)
        for dx in range(NX):
            for dc in range(NC):
                if dx or dc:
                    xx, cc = (x + dx) % NX, (c + dc) % NC
                    rcopy(obuf.at[xx * NC + cc], r1.at[x], r1s, r1r, dev(xx, z, cc, y)).start()
        pltpu.make_async_copy(obuf.at[x * NC + c], r1.at[x], r1r).start()

    wait_bytes(r1, r1r)
    for d in range(1, NZ):
        zz = zm(d)
        rcopy(
            r1.at[:, zz], colout.at[pl.ds(z * 4, 4)], r2s, r2r, dev(x, zz, c, y)
        ).start()
    pltpu.make_async_copy(r1.at[:, z], colout.at[pl.ds(z * 4, 4)], r2r).start()

    wait_bytes(tiles.at[pl.ds(oth * 64, 64)], psem)
    for f in range(2):
        for i in range(PICKS):
            t = lists[0, f, i]
            at = (t % 2) * 64 + t // 2
            fark[i * SUM : (i + 1) * SUM, :] = tiles[at, f, 0]
            farv[i * SUM : (i + 1) * SUM, :] = tiles[at, f, 1]
        for i in range(BLK // QC):
            rs = slice(i * QC, (i + 1) * QC)
            s = dot_t(q[rs, (2 + f) * HD : (3 + f) * HD], fark[...])
            s = jnp.where(jnp.full((QC, BLK), seq, jnp.int32) > 0, s, NEG)
            m0 = m_s[f, rs, :][:, :1]
            m = jnp.maximum(jnp.max(s, axis=1, keepdims=True), m0)
            p = jnp.exp2((s - m) * EXPC)
            shrink = jnp.exp2((m0 - m) * EXPC)
            l = l_s[f, rs, :][:, :1] * shrink + jnp.sum(p, axis=1, keepdims=True)
            acc = acc_s[f, rs, :] * shrink + dot(p.astype(BF), farv[...])
            ofix[f, i * (QC // 8) : (i + 1) * (QC // 8)] = (acc / l).astype(BF).reshape(QC // 8, 8, HD)
        attended_send(1 + f, quarter(ofix.at[f]), f, 1)

    wait_bytes(colout, r2r)
    attended_send(3, quarter(colout), 1, 0)

    wait_bytes(wrows(yl, 1), wrsem.at[1])
    wait_bytes(wrows(yr, 0), wrsem.at[2])
    wait_bytes(wrows(y2, 0), wrsem.at[4])
    wait_bytes(wrows(y2, 1), wrsem.at[5])
    wait_bytes(abuf, asem)
    psends = []
    ap = abuf[oth].reshape(128, 1024)
    for n in range(4):
        pbuf[n] = dot(ap, wbuf[:, n * 512 : (n + 1) * 512]).astype(BF)
        cp = rcopy(pbuf.at[n], prcv.at[n], fsend.at[n], frecv.at[n], partner)
        cp.start()
        psends.append(cp)
    ao = abuf[c].reshape(128, 1024)
    for n in range(4):
        po = dot(ao, wbuf[:, n * 512 : (n + 1) * 512])
        psends[n].wait_recv()
        out[:, n * 512 : (n + 1) * 512] = (po + prcv[n].astype(F32)).astype(BF)

    for cp in psends:
        cp.wait_send()
    for cp in wsends:
        cp.wait_send()
    for cp, tc in ysends:
        if tc is None:
            cp.wait_send()
        else:
            @pl.when(c != tc)
            def _():
                cp.wait_send()
    wait_bytes(tiles.at[pl.ds(0, 127)], tsend)
    wait_bytes(stage.at[:, pl.ds(0, 60)], a2s)
    for dx in range(1, NX):
        p2[dx].wait_send()

    @pl.when(c != OC)
    def _():
        p2[0].wait_send()

    @pl.when(c == OC)
    def _():
        wait_bytes(obuf.at[pl.ds(0, 7)], r1s)

    wait_bytes(r1.at[:, pl.ds(0, 15)], r2s)


NBLK8 = NX * NZ * NC * 8


def per_device(queries, keys, values, summary_lists, out_weight):
    q3, k3, v3 = (a.reshape(64, 8, 512) for a in (queries, keys, values))
    vm = pl.BlockSpec(memory_space=pltpu.VMEM)
    anys = pl.BlockSpec(memory_space=pl.ANY)
    dma = pltpu.SemaphoreType.DMA
    return pl.pallas_call(
        kernel,
        out_shape=jax.ShapeDtypeStruct((128, 2048), BF),
        in_specs=[pl.BlockSpec(memory_space=pltpu.SMEM)] + [vm] * 3 + [anys] * 6,
        out_specs=vm,
        scratch_shapes=[
            pltpu.VMEM((128, 2, 2, SUM, HD), BF),
            pltpu.VMEM((1024, 2048), BF),
            pltpu.VMEM((2, 16, 8, 1024), BF),
            pltpu.VMEM((3, 64, 8, HD), BF),
            pltpu.VMEM((NZ, 3, 4, 8, HD), BF),
            pltpu.VMEM((NX * NC, NZ, 3, 8, HD), BF),
            pltpu.VMEM((NX * NC, NZ, 8, HD), BF),
            pltpu.VMEM((NX, NZ, 8, HD), BF),
            pltpu.VMEM((64, 8, HD), BF),
            pltpu.VMEM((64, 8, HD), BF),
            pltpu.VMEM((2, 64, 8, HD), BF),
            pltpu.VMEM((3, NBLK8, HD), F32),
            pltpu.VMEM((NBLK8, HD), F32),
            pltpu.VMEM((2, BLK, HD), F32),
            pltpu.VMEM((2, BLK, HD), F32),
            pltpu.VMEM((2, BLK, HD), F32),
            pltpu.VMEM((BLK, HD), BF),
            pltpu.VMEM((BLK, HD), BF),
            pltpu.VMEM((4, 128, 512), BF),
            pltpu.VMEM((4, 128, 512), BF),
            dma((8,)), dma((2,)), dma((6,)), dma((6,)), dma, dma((9,)), dma((9,)), dma((16,)), dma((16,)), dma((2,)), dma,
            dma, dma((16,)), dma((4,)), dma, dma, dma, dma, dma, dma((4, 4)), dma, dma((4,)), dma((4,)),
        ],
        compiler_params=pltpu.CompilerParams(
            collective_id=0, has_side_effects=True, vmem_limit_bytes=48 * 1024 * 1024
        ),
    )(summary_lists, queries, keys, values, q3, k3, v3, keys, values, out_weight)


def solution(mesh):
    return jax.shard_map(
        per_device,
        mesh=mesh,
        in_specs=(
            P("seq", "head"),
            P("seq", "head"),
            P("seq", "head"),
            P("seq", "head", None),
            P("head", None),
        ),
        out_specs=P(("seq", "head"), None),
        check_vma=False,
    )
```

```python
import functools
import math

import jax
import jax.numpy as jnp
from jax import lax
from jax.experimental import pallas as pl
from jax.experimental.pallas import tpu as pltpu
from jax.sharding import PartitionSpec as P

MESH = pl.DeviceIdType.MESH
HD = 128
BLK = 512
NX, NZ, NC, NY = 4, 16, 2, 4
PICKS = 16
SUM = 32
NEG = -1e30
EXPC = (HD ** -0.5) * math.log2(math.e)
QC = 256
OC = 0
SENDS = ((8, 7, -7), (6, -6), (5, -5), (4, -4), (3, -3), (2, -2, 1, -1, 0), (), ())
BF = jnp.bfloat16
F32 = jnp.float32


def dot_t(a, b):
    return lax.dot_general(a, b, (((1,), (1,)), ((), ())), preferred_element_type=F32)


def dot(a, b):
    return jnp.dot(a, b, preferred_element_type=F32)


def kernel(
    lists_h, q_h, k_h, v_h, q3, k3, v3, w,
    out,
    lists, q, k, v,
    tiles, wbuf, abuf, stage, c2, obuf, orow, ofix,
    cf, cfo, acc_s, m_s, l_s, fark, farv, pbuf, prcv,
    qsem, lsem, wlsem, wssem, wrsem, tsend, zl, zr, xl, xr, x2sem, psem,
    rowsem, a2s, a2r, r1s, ysend, asem, fsend, frecv,
):
    seq = lax.axis_index("seq")
    y = lax.axis_index("head")
    x = seq // (NZ * NC)
    z = (seq // NC) % NZ
    c = seq % NC
    oth = 1 - c

    def dev(xx, zz, cc, yy):
        return ((xx * NZ + zz) * NC + cc, yy)

    def rcopy(src, dst, ss, rs, to):
        return pltpu.make_async_remote_copy(
            src_ref=src, dst_ref=dst, send_sem=ss, recv_sem=rs, device_id=to, device_id_type=MESH
        )

    def wait_bytes(ref, sem):
        pltpu.make_async_copy(ref, ref, sem).wait()

    loads = []
    for t, (src, dst) in enumerate(((q_h, q), (k_h, k), (v_h, v))):
        loads.append(pltpu.make_async_copy(src, dst, qsem.at[t]))
        loads[-1].start()

    bar = pltpu.get_barrier_semaphore()

    def greet(to):
        pl.semaphore_signal(bar, inc=1, device_id=to, device_id_type=MESH)

    def greet_z(i, carry):
        greet(dev(x, (z + i) % NZ, c, y))
        return carry

    lax.fori_loop(1, NZ, greet_z, 0)
    for dx in range(NX):
        for dc in range(NC):
            if dx or dc:
                greet(dev((x + dx) % NX, z, (c + dc) % NC, y))
    for dy in range(1, NY):
        for dc in range(NC):
            greet(dev(x, z, (c + dc) % NC, (y + dy) % NY))

    own = c * 64 + x * NZ + z
    local = []
    for t, src in enumerate((q3, k3, v3)):
        local.append(pltpu.make_async_copy(src.at[:, :, HD : 2 * HD], stage.at[t], lsem.at[t]))
    local.append(pltpu.make_async_copy(lists_h, lists, lsem.at[8]))
    for f in range(2):
        for t, src in enumerate((k_h, v_h)):
            local.append(
                pltpu.make_async_copy(
                    src.at[BLK - SUM : BLK, (2 + f) * HD : (3 + f) * HD],
                    tiles.at[own, f, t],
                    lsem.at[3 + 2 * f + t],
                )
            )
    for h in range(2):
        local.append(
            pltpu.make_async_copy(
                w.at[pl.ds(pl.multiple_of((2 * h + c) * HD, HD), HD)],
                wbuf.at[pl.ds(pl.multiple_of((y * 2 + h) * HD, HD), HD)],
                wlsem.at[h],
            )
        )
    for cp in local:
        cp.start()

    def own_attention(head, i):
        qi = q[i * QC : (i + 1) * QC, head * HD : (head + 1) * HD]
        n = (i + 1) * QC
        s = dot_t(qi, k[:n, head * HD : (head + 1) * HD])
        rows = lax.broadcasted_iota(jnp.int32, (QC, n), 0) + i * QC
        cols = lax.broadcasted_iota(jnp.int32, (QC, n), 1)
        s = jnp.where(rows >= cols, s, NEG)
        m = jnp.max(s, axis=1, keepdims=True)
        p = jnp.exp2((s - m) * EXPC)
        l = jnp.sum(p, axis=1, keepdims=True)
        acc = dot(p.astype(BF), v[:n, head * HD : (head + 1) * HD])
        return m, l, acc

    for cp in loads:
        cp.wait()
    for i in range(BLK // QC):
        m, l, acc = own_attention(0, i)
        orow[i * (QC // 8) : (i + 1) * (QC // 8)] = (acc / l).astype(BF).reshape(QC // 8, 8, HD)
    for f in range(2):
        for i in range(BLK // QC):
            m, l, acc = own_attention(2 + f, i)
            rs = slice(i * QC, (i + 1) * QC)
            acc_s[f, rs, :] = acc
            m_s[f, rs, :] = jnp.broadcast_to(m, (QC, HD))
            l_s[f, rs, :] = jnp.broadcast_to(l, (QC, HD))

    for cp in local:
        cp.wait()
    pl.semaphore_wait(bar, (NZ - 1) + (NX * NC - 1) + (NY - 1) * NC)
    for dx in range(NX):
        for dc in range(NC):
            if dx or dc:
                pl.semaphore_signal(
                    rowsem, inc=1, device_id=dev((x + dx) % NX, z, (c + dc) % NC, y), device_id_type=MESH
                )

    def wrows(yy, h):
        return wbuf.at[pl.ds(pl.multiple_of((yy * 2 + h) * HD, HD), HD)]

    yr, yl, y2 = (y + 1) % NY, (y + NY - 1) % NY, (y + 2) % NY
    wsends = []

    def wsend(n, yy, h, to, rsem):
        cp = rcopy(wrows(yy, h), wrows(yy, h), wssem.at[n], rsem, dev(x, z, c, to))
        cp.start()
        wsends.append(cp)

    def wsend_first():
        wsend(0, y, 0, yr, wrsem.at[0])
        wsend(1, y, 1, yl, wrsem.at[3])
        wsend(2, y, 1, yr, wrsem.at[1])
        wsend(3, y, 0, yl, wrsem.at[2])

    def wrelay():
        wait_bytes(wrows(yl, 0), wrsem.at[0])
        wsend(4, yl, 0, yr, wrsem.at[4])
        wait_bytes(wrows(yr, 1), wrsem.at[3])
        wsend(5, yr, 1, yl, wrsem.at[5])

    ysends = []

    def attended_send(n, src_of, tc, h):
        lanes = pl.ds(pl.multiple_of((y * 2 + h) * HD, HD), HD)
        dst = abuf.at[c, :, :, lanes]
        for dy in range(1, NY):
            yy = (y + dy) % NY
            cp = rcopy(src_of(yy), dst, ysend.at[n, dy], asem, dev(x, z, tc, yy))
            cp.start()
            ysends.append((cp, None))
        near = rcopy(src_of(y), dst, ysend.at[n, 0], asem, dev(x, z, oth, y))
        ysends.append((near, tc))

        @pl.when(c == tc)
        def _():
            pltpu.make_async_copy(src_of(y), dst, asem).start()

        @pl.when(c != tc)
        def _():
            near.start()

    def quarter(ref):
        return lambda yy: ref.at[pl.ds(pl.multiple_of(yy * 16, 16), 16)]

    xr_, xl_, x2_ = (x + 1) % NX, (x + NX - 1) % NX, (x + 2) % NX

    def slot(xx, zz):
        return c * 64 + xx * NZ + zz

    def zm(d):
        return (z + d + NZ) % NZ

    def tsend_to(src, rs, to):
        rcopy(src, src, tsend, rs, to).start()

    def ring_send(s):
        right, left = dev(x, zm(1), c, y), dev(x, zm(-1), c, y)
        if s < 8:
            tsend_to(tiles.at[slot(x, zm(1 - s))], zl.at[s], right)
            tsend_to(tiles.at[slot(x, zm(s - 1))], zr.at[s], left)
        else:
            tsend_to(tiles.at[slot(x, zm(-7)), 0], zl.at[8], right)
            tsend_to(tiles.at[slot(x, zm(7)), 1], zr.at[8], left)

    def ring_wait(s):
        if s < 8:
            wait_bytes(tiles.at[slot(x, zm(-s))], zl.at[s])
            wait_bytes(tiles.at[slot(x, zm(s))], zr.at[s])
        else:
            wait_bytes(tiles.at[slot(x, zm(8)), 0], zl.at[8])
            wait_bytes(tiles.at[slot(x, zm(8)), 1], zr.at[8])

    def members(n):
        if n == 0:
            return [z]
        if n == 8:
            return [zm(8)]
        return [zm(-n), zm(n)]

    partner = dev(x, z, oth, y)

    def forward(n):
        for zz in members(n):
            src = tiles.at[slot(x, zz)]
            tsend_to(src, xl.at[zz], dev(xr_, z, c, y))
            tsend_to(src, xr.at[zz], dev(xl_, z, c, y))
            tsend_to(src, psem, partner)

    def relay(n):
        for zz in members(n):
            src = tiles.at[slot(xl_, zz)]
            wait_bytes(src, xl.at[zz])
            tsend_to(src.at[0], x2sem.at[0], dev(xr_, z, c, y))
            tsend_to(src, psem, partner)
            src = tiles.at[slot(xr_, zz)]
            wait_bytes(src, xr.at[zz])
            tsend_to(src.at[1], x2sem.at[1], dev(xl_, z, c, y))
            tsend_to(src, psem, partner)

    src_id = x * NC + c

    def col_send(d):
        zz = zm(d)
        for dx in range(NX):
            g = (x + dx) % NX
            cp = rcopy(stage.at[:, zz * 4 + g], c2.at[src_id, z], a2s, a2r, dev(g, zz, OC, y))
            if d or dx:
                cp.start()
            else:

                @pl.when(c == OC)
                def _():
                    pltpu.make_async_copy(stage.at[:, zz * 4 + g], c2.at[src_id, z], a2r).start()

                @pl.when(c != OC)
                def _():
                    cp.start()

    pl.semaphore_wait(rowsem, NX * NC - 1)
    wsend_first()
    for s in range(1, 9):
        ring_send(s)
        for d in SENDS[s - 1]:
            col_send(d)
        forward(s - 1)
        if s >= 2:
            relay(s - 2)
        if s == 2:
            attended_send(0, quarter(orow), 0, 0)
        if s == 6:
            wrelay()
        ring_wait(s)
    forward(8)

    relay(7)

    @pl.when(c == OC)
    def _():
        wait_bytes(c2, a2r)
        for t in range(3):
            cf[t] = c2[:, :, t].astype(F32).reshape(NBLK8, HD)

        def blk(r):
            return (r // 32) * 32 + (r % 16) * 2 + (r // 16) % 2

        rq = blk(lax.broadcasted_iota(jnp.int32, (128, 128), 0))
        rk = blk(lax.broadcasted_iota(jnp.int32, (128, 128), 1))
        ok = rq >= rk
        for j in range(8):
            cols = pl.ds(j, 128, stride=8)
            qc = cf[0, cols, :].astype(BF)
            kc = cf[1, cols, :].astype(BF)
            vc = cf[2, cols, :].astype(BF)
            s = jnp.where(ok, dot_t(qc, kc), NEG)
            m = jnp.max(s, axis=1, keepdims=True)
            p = jnp.exp2((s - m) * EXPC)
            l = jnp.sum(p, axis=1, keepdims=True)
            cfo[cols, :] = dot(p.astype(BF), vc) / l
        obuf[...] = cfo[...].astype(BF).reshape(NX, NC, NZ, 8, HD)
        lanes = pl.ds(pl.multiple_of(y * 2 * HD, HD), HD)

        def give_back(i, carry):
            for dx in range(NX):
                xx, zz = (x + dx) % NX, (z + i) % NZ
                rcopy(
                    obuf.at[xx, :, zz], abuf.at[:, (z % 4) * 4 + x, :, lanes], r1s, asem, dev(xx, zz, 1, z // 4)
                ).start()
            return carry

        lax.fori_loop(0, NZ, give_back, 0)

    relay(8)
    far2 = tiles.at[pl.ds(slot(x2_, 0), NZ)]
    wait_bytes(far2.at[:, 0], x2sem.at[0])
    wait_bytes(far2.at[:, 1], x2sem.at[1])
    tsend_to(far2, psem, partner)

    wait_bytes(tiles.at[pl.ds(oth * 64, 64)], psem)
    for f in range(2):
        for i in range(PICKS):
            t = lists[0, f, i]
            at = (t % 2) * 64 + t // 2
            fark[i * SUM : (i + 1) * SUM, :] = tiles[at, f, 0]
            farv[i * SUM : (i + 1) * SUM, :] = tiles[at, f, 1]
        for i in range(BLK // QC):
            rs = slice(i * QC, (i + 1) * QC)
            s = dot_t(q[rs, (2 + f) * HD : (3 + f) * HD], fark[...])
            s = jnp.where(jnp.full((QC, BLK), seq, jnp.int32) > 0, s, NEG)
            m0 = m_s[f, rs, :][:, :1]
            m = jnp.maximum(jnp.max(s, axis=1, keepdims=True), m0)
            p = jnp.exp2((s - m) * EXPC)
            shrink = jnp.exp2((m0 - m) * EXPC)
            l = l_s[f, rs, :][:, :1] * shrink + jnp.sum(p, axis=1, keepdims=True)
            acc = acc_s[f, rs, :] * shrink + dot(p.astype(BF), farv[...])
            ofix[f, i * (QC // 8) : (i + 1) * (QC // 8)] = (acc / l).astype(BF).reshape(QC // 8, 8, HD)
        attended_send(1 + f, quarter(ofix.at[f]), f, 1)


    wait_bytes(wrows(yl, 1), wrsem.at[1])
    wait_bytes(wrows(yr, 0), wrsem.at[2])
    wait_bytes(wrows(y2, 0), wrsem.at[4])
    wait_bytes(wrows(y2, 1), wrsem.at[5])
    wait_bytes(abuf, asem)
    psends = []
    ap = abuf[oth].reshape(128, 1024)
    for n in range(4):
        pbuf[n] = dot(ap, wbuf[:, n * 512 : (n + 1) * 512]).astype(BF)
        cp = rcopy(pbuf.at[n], prcv.at[n], fsend.at[n], frecv.at[n], partner)
        cp.start()
        psends.append(cp)
    ao = abuf[c].reshape(128, 1024)
    for n in range(4):
        po = dot(ao, wbuf[:, n * 512 : (n + 1) * 512])
        psends[n].wait_recv()
        out[:, n * 512 : (n + 1) * 512] = (po + prcv[n].astype(F32)).astype(BF)

    for cp in psends:
        cp.wait_send()
    for cp in wsends:
        cp.wait_send()
    for cp, tc in ysends:
        if tc is None:
            cp.wait_send()
        else:
            @pl.when(c != tc)
            def _():
                cp.wait_send()
    wait_bytes(tiles.at[pl.ds(0, 127)], tsend)

    @pl.when(c != OC)
    def _():
        wait_bytes(stage, a2s)

    @pl.when(c == OC)
    def _():
        wait_bytes(stage.at[:, pl.ds(0, 63)], a2s)
        wait_bytes(obuf, r1s)


NBLK8 = NX * NZ * NC * 8


def per_device(queries, keys, values, summary_lists, out_weight):
    q3, k3, v3 = (a.reshape(64, 8, 512) for a in (queries, keys, values))
    vm = pl.BlockSpec(memory_space=pltpu.VMEM)
    anys = pl.BlockSpec(memory_space=pl.ANY)
    dma = pltpu.SemaphoreType.DMA
    return pl.pallas_call(
        kernel,
        out_shape=jax.ShapeDtypeStruct((128, 2048), BF),
        in_specs=[anys] * 8,
        out_specs=vm,
        scratch_shapes=[
            pltpu.SMEM((1, 2, PICKS), jnp.int32),
            pltpu.VMEM((BLK, 512), BF),
            pltpu.VMEM((BLK, 512), BF),
            pltpu.VMEM((BLK, 512), BF),
            pltpu.VMEM((128, 2, 2, SUM, HD), BF),
            pltpu.VMEM((1024, 2048), BF),
            pltpu.VMEM((2, 16, 8, 1024), BF),
            pltpu.VMEM((3, 64, 8, HD), BF),
            pltpu.VMEM((NX * NC, NZ, 3, 8, HD), BF),
            pltpu.VMEM((NX, NC, NZ, 8, HD), BF),
            pltpu.VMEM((64, 8, HD), BF),
            pltpu.VMEM((2, 64, 8, HD), BF),
            pltpu.VMEM((3, NBLK8, HD), F32),
            pltpu.VMEM((NBLK8, HD), F32),
            pltpu.VMEM((2, BLK, HD), F32),
            pltpu.VMEM((2, BLK, HD), F32),
            pltpu.VMEM((2, BLK, HD), F32),
            pltpu.VMEM((BLK, HD), BF),
            pltpu.VMEM((BLK, HD), BF),
            pltpu.VMEM((4, 128, 512), BF),
            pltpu.VMEM((4, 128, 512), BF),
            dma((3,)), dma((9,)), dma((2,)), dma((6,)), dma((6,)), dma, dma((9,)), dma((9,)), dma((16,)), dma((16,)), dma((2,)), dma,
            pltpu.SemaphoreType.REGULAR, dma, dma, dma, dma((3, 4)), dma, dma((4,)), dma((4,)),
        ],
        compiler_params=pltpu.CompilerParams(
            collective_id=0, has_side_effects=True, vmem_limit_bytes=67043328
        ),
    )(summary_lists, queries, keys, values, q3, k3, v3, out_weight)


def solution(mesh):
    return jax.shard_map(
        per_device,
        mesh=mesh,
        in_specs=(
            P("seq", "head"),
            P("seq", "head"),
            P("seq", "head"),
            P("seq", "head", None),
            P("head", None),
        ),
        out_specs=P(("seq", "head"), None),
        check_vma=False,
    )
```

```python
import functools
import math

import jax
import jax.numpy as jnp
from jax import lax
from jax.experimental import pallas as pl
from jax.experimental.pallas import tpu as pltpu
from jax.sharding import PartitionSpec as P

MESH = pl.DeviceIdType.MESH
HD = 128
BLK = 512
NX, NZ, NC, NY = 4, 16, 2, 4
PICKS = 16
SUM = 32
NEG = -1e30
EXPC = (HD ** -0.5) * math.log2(math.e)
QC = 256
OC = 0
ZGROUPS = ((0,), (-5, 5, -1, 1), (-6, 6, -4, 4, -2, 2), (-7, 7, -3, 3), (8,))
ZSENDS = (
    ((0, 5, None), (0, -5, None), (0, 1, None), (0, -1, None)),
    ((-5, 1, None), (5, -1, None), (-5, -1, None), (5, 1, None), (-1, 1, None), (1, -1, None)),
    ((-6, 1, None), (6, -1, None), (-4, -1, None), (4, 1, None)),
    ((-7, 1, 0), (7, -1, 1)),
)
SENDS = ((8, 0, 1, -1), (7, -7, 6, -6), (5, -5, 4, -4), (3, -3, 2, -2))
BF = jnp.bfloat16
F32 = jnp.float32


def dot_t(a, b):
    return lax.dot_general(a, b, (((1,), (1,)), ((), ())), preferred_element_type=F32)


def dot(a, b):
    return jnp.dot(a, b, preferred_element_type=F32)


def kernel(
    lists_h, q_h, k_h, v_h, q3, k3, v3, w,
    out,
    lists, q, k, v,
    tiles, wbuf, abuf, part, stage, c2, obuf, orow, ofix,
    cf, cfo, acc_s, m_s, l_s, fark, farv, pbuf, prcv,
    qsem, lsem, wlsem, wssem, wrsem, tsend, zsem, xl, xr, x2sem, psem,
    rowsem, a2s, a2r, r1s, ysend, asem, fsend, frecv,
):
    seq = lax.axis_index("seq")
    y = lax.axis_index("head")
    x = seq // (NZ * NC)
    z = (seq // NC) % NZ
    c = seq % NC
    oth = 1 - c

    def dev(xx, zz, cc, yy):
        return ((xx * NZ + zz) * NC + cc, yy)

    def rcopy(src, dst, ss, rs, to):
        return pltpu.make_async_remote_copy(
            src_ref=src, dst_ref=dst, send_sem=ss, recv_sem=rs, device_id=to, device_id_type=MESH
        )

    def wait_bytes(ref, sem):
        pltpu.make_async_copy(ref, ref, sem).wait()

    loads = []
    for t, (src, dst) in enumerate(((q_h, q), (k_h, k), (v_h, v))):
        loads.append(pltpu.make_async_copy(src, dst, qsem.at[t]))
        loads[-1].start()

    bar = pltpu.get_barrier_semaphore()

    def greet(to):
        pl.semaphore_signal(bar, inc=1, device_id=to, device_id_type=MESH)

    def greet_z(i, carry):
        greet(dev(x, (z + i) % NZ, c, y))
        return carry

    lax.fori_loop(1, NZ, greet_z, 0)
    for dx in range(NX):
        for dc in range(NC):
            if dx or dc:
                greet(dev((x + dx) % NX, z, (c + dc) % NC, y))
    for dy in range(1, NY):
        for dc in range(NC):
            greet(dev(x, z, (c + dc) % NC, (y + dy) % NY))

    own = c * 64 + x * NZ + z
    local = []
    for t, src in enumerate((q3, k3, v3)):
        local.append(pltpu.make_async_copy(src.at[:, :, HD : 2 * HD], stage.at[:, t], lsem.at[t]))
    local.append(pltpu.make_async_copy(lists_h, lists, lsem.at[8]))
    for f in range(2):
        for t, src in enumerate((k_h, v_h)):
            local.append(
                pltpu.make_async_copy(
                    src.at[BLK - SUM : BLK, (2 + f) * HD : (3 + f) * HD],
                    tiles.at[own, f, t],
                    lsem.at[3 + 2 * f + t],
                )
            )
    for h in range(2):
        local.append(
            pltpu.make_async_copy(
                w.at[pl.ds(pl.multiple_of((2 - c if h else 3 * c) * HD, HD), HD)],
                wbuf.at[pl.ds(pl.multiple_of((h * NY + y) * HD, HD), HD)],
                wlsem.at[h],
            )
        )
    for cp in local:
        cp.start()

    def own_attention(head, i):
        qi = q[i * QC : (i + 1) * QC, head * HD : (head + 1) * HD]
        n = (i + 1) * QC
        s = dot_t(qi, k[:n, head * HD : (head + 1) * HD])
        rows = lax.broadcasted_iota(jnp.int32, (QC, n), 0) + i * QC
        cols = lax.broadcasted_iota(jnp.int32, (QC, n), 1)
        s = jnp.where(rows >= cols, s, NEG)
        m = jnp.max(s, axis=1, keepdims=True)
        p = jnp.exp2((s - m) * EXPC)
        l = jnp.sum(p, axis=1, keepdims=True)
        acc = dot(p.astype(BF), v[:n, head * HD : (head + 1) * HD])
        return m, l, acc

    for cp in loads:
        cp.wait()
    for i in range(BLK // QC):
        m, l, acc = own_attention(0, i)
        orow[i * (QC // 8) : (i + 1) * (QC // 8)] = (acc / l).astype(BF).reshape(QC // 8, 8, HD)
    for f in range(2):
        for i in range(BLK // QC):
            m, l, acc = own_attention(2 + f, i)
            rs = slice(i * QC, (i + 1) * QC)
            acc_s[f, rs, :] = acc
            m_s[f, rs, :] = jnp.broadcast_to(m, (QC, HD))
            l_s[f, rs, :] = jnp.broadcast_to(l, (QC, HD))

    for cp in local:
        cp.wait()
    pl.semaphore_wait(bar, (NZ - 1) + (NX * NC - 1) + (NY - 1) * NC)
    for dx in range(NX):
        for dc in range(NC):
            if dx or dc:
                pl.semaphore_signal(
                    rowsem, inc=1, device_id=dev((x + dx) % NX, z, (c + dc) % NC, y), device_id_type=MESH
                )

    def wrows(yy, h):
        return wbuf.at[pl.ds(pl.multiple_of((h * NY + yy) * HD, HD), HD)]

    yr, yl, y2 = (y + 1) % NY, (y + NY - 1) % NY, (y + 2) % NY
    wsends = []

    def wsend(n, yy, h, to, rsem):
        cp = rcopy(wrows(yy, h), wrows(yy, h), wssem.at[n], rsem, dev(x, z, c, to))
        cp.start()
        wsends.append(cp)

    def wsend_first():
        wsend(0, y, 0, yr, wrsem.at[0])
        wsend(1, y, 1, yl, wrsem.at[3])
        wsend(2, y, 1, yr, wrsem.at[1])
        wsend(3, y, 0, yl, wrsem.at[2])

    def wrelay():
        wait_bytes(wrows(yl, 0), wrsem.at[0])
        wsend(4, yl, 0, yr, wrsem.at[4])
        wait_bytes(wrows(yr, 1), wrsem.at[3])
        wsend(5, yr, 1, yl, wrsem.at[5])

    ysends = []

    def attended_send(n, src_of, tc, h):
        dst = abuf.at[h, c, :, :, pl.ds(pl.multiple_of(y * HD, HD), HD)]
        for dy in range(1, NY):
            yy = (y + dy) % NY
            cp = rcopy(src_of(yy), dst, ysend.at[n, dy], asem.at[h], dev(x, z, tc, yy))
            cp.start()
            ysends.append((cp, None))
        near = rcopy(src_of(y), dst, ysend.at[n, 0], asem.at[h], dev(x, z, oth, y))
        ysends.append((near, tc))

        @pl.when(c == tc)
        def _():
            pltpu.make_async_copy(src_of(y), dst, asem.at[h]).start()

        @pl.when(c != tc)
        def _():
            near.start()

    def quarter(ref):
        return lambda yy: ref.at[pl.ds(pl.multiple_of(yy * 16, 16), 16)]

    xr_, xl_, x2_ = (x + 1) % NX, (x + NX - 1) % NX, (x + 2) % NX

    def slot(xx, zz):
        return c * 64 + xx * NZ + zz

    def zm(d):
        return (z + d + NZ) % NZ

    def tsend_to(src, rs, to):
        rcopy(src, src, tsend, rs, to).start()

    def zcopies(step):
        for rel, dz, half in ZSENDS[step]:
            src = tiles.at[slot(x, zm(rel))]
            if half is not None:
                src = src.at[half]
            tsend_to(src, zsem.at[(rel - dz) % NZ if half != 1 else 0], dev(x, zm(dz), c, y))

    def zwait(group):
        for rel in ZGROUPS[group]:
            src = tiles.at[slot(x, zm(rel))]
            if rel == 8:
                wait_bytes(src.at[0], zsem.at[8])
                wait_bytes(src.at[1], zsem.at[0])
            else:
                wait_bytes(src, zsem.at[rel % NZ])

    def members(n):
        return [zm(rel) for rel in ZGROUPS[n]]

    partner = dev(x, z, oth, y)

    def forward(n):
        for zz in members(n):
            src = tiles.at[slot(x, zz)]
            tsend_to(src, xl.at[zz], dev(xr_, z, c, y))
            tsend_to(src, xr.at[zz], dev(xl_, z, c, y))
            tsend_to(src, psem, partner)
            if n == 4:
                tsend_to(src.at[0], x2sem.at[0], dev(x2_, z, c, y))
                tsend_to(src.at[1], x2sem.at[1], dev(x2_, z, c, y))

    def relay(n):
        for zz in members(n):
            src = tiles.at[slot(xl_, zz)]
            wait_bytes(src, xl.at[zz])
            if n < 4:
                tsend_to(src.at[0], x2sem.at[0], dev(xr_, z, c, y))
            tsend_to(src, psem, partner)
            src = tiles.at[slot(xr_, zz)]
            wait_bytes(src, xr.at[zz])
            if n < 4:
                tsend_to(src.at[1], x2sem.at[1], dev(xl_, z, c, y))
            tsend_to(src, psem, partner)

    src_id = x * NC + c

    def col_send(d):
        zz = zm(d)
        for dx in range(NX):
            g = (x + dx) % NX
            cp = rcopy(stage.at[zz * 4 + g], c2.at[src_id, z], a2s, a2r, dev(g, zz, OC, y))
            if d or dx:
                cp.start()
            else:

                @pl.when(c == OC)
                def _():
                    pltpu.make_async_copy(stage.at[zz * 4 + g], c2.at[src_id, z], a2r).start()

                @pl.when(c != OC)
                def _():
                    cp.start()

    wsend_first()
    for n in range(4):
        if n:
            zwait(n)
        zcopies(n)
        forward(n)
        if n == 0:
            pl.semaphore_wait(rowsem, NX * NC - 1)
        for d in SENDS[n]:
            col_send(d)
        if n >= 1:
            relay(n - 1)
        if n == 1:
            attended_send(0, quarter(orow), 0, 0)
        if n == 2:
            wrelay()
    zwait(4)
    forward(4)
    relay(3)
    relay(4)
    far2 = tiles.at[pl.ds(slot(x2_, 0), NZ)]
    wait_bytes(far2.at[:, 0], x2sem.at[0])
    wait_bytes(far2.at[:, 1], x2sem.at[1])
    tsend_to(far2, psem, partner)

    @pl.when(c == OC)
    def _():
        wait_bytes(c2, a2r)
        for t in range(3):
            cf[t] = c2[:, :, t].astype(F32).reshape(NBLK8, HD)

        def blk(r):
            return (r // 32) * 32 + (r % 16) * 2 + (r // 16) % 2

        rq = blk(lax.broadcasted_iota(jnp.int32, (128, 128), 0))
        rk = blk(lax.broadcasted_iota(jnp.int32, (128, 128), 1))
        ok = rq >= rk
        for j in range(8):
            cols = pl.ds(j, 128, stride=8)
            qc = cf[0, cols, :].astype(BF)
            kc = cf[1, cols, :].astype(BF)
            vc = cf[2, cols, :].astype(BF)
            s = jnp.where(ok, dot_t(qc, kc), NEG)
            m = jnp.max(s, axis=1, keepdims=True)
            p = jnp.exp2((s - m) * EXPC)
            l = jnp.sum(p, axis=1, keepdims=True)
            cfo[cols, :] = dot(p.astype(BF), vc) / l
        back = cfo[...].astype(BF).reshape(NX, NC, NZ, 8, HD)
        for cc in range(NC):
            obuf[:, :, cc] = back[:, cc]
        lanes = pl.ds(pl.multiple_of(y * HD, HD), HD)

        def give_back(i, carry):
            for zz in ((z + 8 - i) % NZ, (z + NZ - 7 + i) % NZ):
                for dx in range(NX):
                    xx = (x + dx) % NX
                    rcopy(
                        obuf.at[xx, zz],
                        abuf.at[1, :, (z % 4) * 4 + x, :, lanes],
                        r1s,
                        asem.at[1],
                        dev(xx, zz, 1, z // 4),
                    ).start()
            return carry

        lax.fori_loop(0, NZ // 2, give_back, 0)

    wait_bytes(tiles.at[pl.ds(oth * 64, 64)], psem)
    for f in range(2):
        for i in range(PICKS):
            t = lists[0, f, i]
            at = (t % 2) * 64 + t // 2
            fark[i * SUM : (i + 1) * SUM, :] = tiles[at, f, 0]
            farv[i * SUM : (i + 1) * SUM, :] = tiles[at, f, 1]
        for i in range(BLK // QC):
            rs = slice(i * QC, (i + 1) * QC)
            s = dot_t(q[rs, (2 + f) * HD : (3 + f) * HD], fark[...])
            s = jnp.where(jnp.full((QC, BLK), seq, jnp.int32) > 0, s, NEG)
            m0 = m_s[f, rs, :][:, :1]
            m = jnp.maximum(jnp.max(s, axis=1, keepdims=True), m0)
            p = jnp.exp2((s - m) * EXPC)
            shrink = jnp.exp2((m0 - m) * EXPC)
            l = l_s[f, rs, :][:, :1] * shrink + jnp.sum(p, axis=1, keepdims=True)
            acc = acc_s[f, rs, :] * shrink + dot(p.astype(BF), farv[...])
            ofix[f, i * (QC // 8) : (i + 1) * (QC // 8)] = (acc / l).astype(BF).reshape(QC // 8, 8, HD)
        attended_send(1 + f, quarter(ofix.at[f]), f, 1 - f)


    wait_bytes(wrows(yr, 0), wrsem.at[2])
    wait_bytes(wrows(y2, 0), wrsem.at[4])
    wait_bytes(abuf.at[0], asem.at[0])
    for i, at in enumerate((oth, c)):
        a = abuf[0, at].reshape(128, 512)
        for n in range(4):
            part[i, :, n * 512 : (n + 1) * 512] = dot(a, wbuf[:512, n * 512 : (n + 1) * 512])
    wait_bytes(wrows(yl, 1), wrsem.at[1])
    wait_bytes(wrows(y2, 1), wrsem.at[5])
    wait_bytes(abuf.at[1], asem.at[1])
    psends = []
    ap = abuf[1, oth].reshape(128, 512)
    for n in range(4):
        cols = slice(n * 512, (n + 1) * 512)
        pbuf[n] = (part[0, :, cols] + dot(ap, wbuf[512:, cols])).astype(BF)
        cp = rcopy(pbuf.at[n], prcv.at[n], fsend.at[n], frecv.at[n], partner)
        cp.start()
        psends.append(cp)
    ao = abuf[1, c].reshape(128, 512)
    for n in range(4):
        cols = slice(n * 512, (n + 1) * 512)
        po = part[1, :, cols] + dot(ao, wbuf[512:, cols])
        psends[n].wait_recv()
        out[:, cols] = (po + prcv[n].astype(F32)).astype(BF)

    for cp in psends:
        cp.wait_send()
    for cp in wsends:
        cp.wait_send()
    for cp, tc in ysends:
        if tc is None:
            cp.wait_send()
        else:
            @pl.when(c != tc)
            def _():
                cp.wait_send()
    wait_bytes(tiles.at[pl.ds(0, 127)], tsend)

    @pl.when(c != OC)
    def _():
        wait_bytes(stage, a2s)

    @pl.when(c == OC)
    def _():
        wait_bytes(stage.at[pl.ds(0, 63)], a2s)
        wait_bytes(obuf, r1s)


NBLK8 = NX * NZ * NC * 8


def per_device(queries, keys, values, summary_lists, out_weight):
    q3, k3, v3 = (a.reshape(64, 8, 512) for a in (queries, keys, values))
    vm = pl.BlockSpec(memory_space=pltpu.VMEM)
    anys = pl.BlockSpec(memory_space=pl.ANY)
    dma = pltpu.SemaphoreType.DMA
    return pl.pallas_call(
        kernel,
        out_shape=jax.ShapeDtypeStruct((128, 2048), BF),
        in_specs=[anys] * 8,
        out_specs=vm,
        scratch_shapes=[
            pltpu.SMEM((1, 2, PICKS), jnp.int32),
            pltpu.VMEM((BLK, 512), BF),
            pltpu.VMEM((BLK, 512), BF),
            pltpu.VMEM((BLK, 512), BF),
            pltpu.VMEM((128, 2, 2, SUM, HD), BF),
            pltpu.VMEM((1024, 2048), BF),
            pltpu.VMEM((2, 2, 16, 8, 512), BF),
            pltpu.VMEM((2, 128, 2048), F32),
            pltpu.VMEM((64, 3, 8, HD), BF),
            pltpu.VMEM((NX * NC, NZ, 3, 8, HD), BF),
            pltpu.VMEM((NX, NZ, NC, 8, HD), BF),
            pltpu.VMEM((64, 8, HD), BF),
            pltpu.VMEM((2, 64, 8, HD), BF),
            pltpu.VMEM((3, NBLK8, HD), F32),
            pltpu.VMEM((NBLK8, HD), F32),
            pltpu.VMEM((2, BLK, HD), F32),
            pltpu.VMEM((2, BLK, HD), F32),
            pltpu.VMEM((2, BLK, HD), F32),
            pltpu.VMEM((BLK, HD), BF),
            pltpu.VMEM((BLK, HD), BF),
            pltpu.VMEM((4, 128, 512), BF),
            pltpu.VMEM((4, 128, 512), BF),
            dma((3,)), dma((9,)), dma((2,)), dma((6,)), dma((6,)), dma, dma((16,)), dma((16,)), dma((16,)), dma((2,)), dma,
            pltpu.SemaphoreType.REGULAR, dma, dma, dma, dma((3, 4)), dma((2,)), dma((4,)), dma((4,)),
        ],
        compiler_params=pltpu.CompilerParams(
            collective_id=0, has_side_effects=True, vmem_limit_bytes=67043328
        ),
    )(summary_lists, queries, keys, values, q3, k3, v3, out_weight)


def solution(mesh):
    return jax.shard_map(
        per_device,
        mesh=mesh,
        in_specs=(
            P("seq", "head"),
            P("seq", "head"),
            P("seq", "head"),
            P("seq", "head", None),
            P("head", None),
        ),
        out_specs=P(("seq", "head"), None),
        check_vma=False,
    )
```

```python
import functools
import math

import jax
import jax.numpy as jnp
from jax import lax
from jax.experimental import pallas as pl
from jax.experimental.pallas import tpu as pltpu
from jax.sharding import PartitionSpec as P

MESH = pl.DeviceIdType.MESH
HD = 128
BLK = 512
NX, NZ, NC, NY = 4, 16, 2, 4
PICKS = 16
SUM = 32
NEG = -1e30
EXPC = (HD ** -0.5) * math.log2(math.e)
QC = 256
OC = 0
ZGROUPS = ((0,), (-5, 5, -1, 1), (-6, 6, -4, 4, -2, 2), (-7, 7, -3, 3), (8,))
ZSENDS = (
    ((0, 5, None), (0, -5, None), (0, 1, None), (0, -1, None)),
    ((-5, 1, None), (5, -1, None), (-5, -1, None), (5, 1, None), (-1, 1, None), (1, -1, None)),
    ((-6, 1, None), (6, -1, None), (-4, -1, None), (4, 1, None)),
    ((-7, 1, 0), (7, -1, 1)),
)
SENDS = ((8,7,-7,0),(6,-6,5,-5,4,-4),(3,-3,2,-2,1,-1),())
BF = jnp.bfloat16
F32 = jnp.float32


def dot_t(a, b):
    return lax.dot_general(a, b, (((1,), (1,)), ((), ())), preferred_element_type=F32)


def dot(a, b):
    return jnp.dot(a, b, preferred_element_type=F32)


def kernel(
    lists_h, q_h, k_h, v_h, q3, k3, v3, w,
    out,
    lists, q, k, v,
    tiles, wbuf, abuf, part, stage, c2, obuf, orow, ofix,
    cf, cfo, acc_s, m_s, l_s, fark, farv, pbuf, prcv,
    qsem, lsem, wlsem, wssem, wrsem, tsend, zsem, xl, xr, x2sem, psem,
    rowsem, a2s, a2r, r1s, ysend, asem, fsend, frecv,
):
    seq = lax.axis_index("seq")
    y = lax.axis_index("head")
    x = seq // (NZ * NC)
    z = (seq // NC) % NZ
    c = seq % NC
    oth = 1 - c

    def dev(xx, zz, cc, yy):
        return ((xx * NZ + zz) * NC + cc, yy)

    def rcopy(src, dst, ss, rs, to):
        return pltpu.make_async_remote_copy(
            src_ref=src, dst_ref=dst, send_sem=ss, recv_sem=rs, device_id=to, device_id_type=MESH
        )

    def wait_bytes(ref, sem):
        pltpu.make_async_copy(ref, ref, sem).wait()

    loads = []
    for t, (src, dst) in enumerate(((q_h, q), (k_h, k), (v_h, v))):
        loads.append(pltpu.make_async_copy(src, dst, qsem.at[t]))
        loads[-1].start()

    bar = pltpu.get_barrier_semaphore()

    def greet(to):
        pl.semaphore_signal(bar, inc=1, device_id=to, device_id_type=MESH)

    def greet_z(i, carry):
        greet(dev(x, (z + i) % NZ, c, y))
        return carry

    lax.fori_loop(1, NZ, greet_z, 0)
    for dx in range(NX):
        for dc in range(NC):
            if dx or dc:
                greet(dev((x + dx) % NX, z, (c + dc) % NC, y))
    for dy in range(1, NY):
        for dc in range(NC):
            greet(dev(x, z, (c + dc) % NC, (y + dy) % NY))

    own = c * 64 + x * NZ + z
    local = []
    for t, src in enumerate((q3, k3, v3)):
        local.append(pltpu.make_async_copy(src.at[:, :, HD : 2 * HD], stage.at[:, t], lsem.at[t]))
    local.append(pltpu.make_async_copy(lists_h, lists, lsem.at[8]))
    for f in range(2):
        for t, src in enumerate((k_h, v_h)):
            local.append(
                pltpu.make_async_copy(
                    src.at[BLK - SUM : BLK, (2 + f) * HD : (3 + f) * HD],
                    tiles.at[own, f, t],
                    lsem.at[3 + 2 * f + t],
                )
            )
    for h in range(2):
        local.append(
            pltpu.make_async_copy(
                w.at[pl.ds(pl.multiple_of((2 - c if h else 3 * c) * HD, HD), HD)],
                wbuf.at[pl.ds(pl.multiple_of((h * NY + y) * HD, HD), HD)],
                wlsem.at[h],
            )
        )
    for cp in local:
        cp.start()

    def own_attention(head, i):
        qi = q[i * QC : (i + 1) * QC, head * HD : (head + 1) * HD]
        n = (i + 1) * QC
        s = dot_t(qi, k[:n, head * HD : (head + 1) * HD])
        rows = lax.broadcasted_iota(jnp.int32, (QC, n), 0) + i * QC
        cols = lax.broadcasted_iota(jnp.int32, (QC, n), 1)
        s = jnp.where(rows >= cols, s, NEG)
        m = jnp.max(s, axis=1, keepdims=True)
        p = jnp.exp2((s - m) * EXPC)
        l = jnp.sum(p, axis=1, keepdims=True)
        acc = dot(p.astype(BF), v[:n, head * HD : (head + 1) * HD])
        return m, l, acc

    for cp in loads:
        cp.wait()
    for i in range(BLK // QC):
        m, l, acc = own_attention(0, i)
        orow[i * (QC // 8) : (i + 1) * (QC // 8)] = (acc / l).astype(BF).reshape(QC // 8, 8, HD)
    for f in range(2):
        for i in range(BLK // QC):
            m, l, acc = own_attention(2 + f, i)
            rs = slice(i * QC, (i + 1) * QC)
            acc_s[f, rs, :] = acc
            m_s[f, rs, :] = jnp.broadcast_to(m, (QC, HD))
            l_s[f, rs, :] = jnp.broadcast_to(l, (QC, HD))

    for cp in local:
        cp.wait()
    pl.semaphore_wait(bar, (NZ - 1) + (NX * NC - 1) + (NY - 1) * NC)
    for dx in range(NX):
        for dc in range(NC):
            if dx or dc:
                pl.semaphore_signal(
                    rowsem, inc=1, device_id=dev((x + dx) % NX, z, (c + dc) % NC, y), device_id_type=MESH
                )

    def wrows(yy, h):
        return wbuf.at[pl.ds(pl.multiple_of((h * NY + yy) * HD, HD), HD)]

    yr, yl, y2 = (y + 1) % NY, (y + NY - 1) % NY, (y + 2) % NY
    wsends = []

    def wsend(n, yy, h, to, rsem):
        cp = rcopy(wrows(yy, h), wrows(yy, h), wssem.at[n], rsem, dev(x, z, c, to))
        cp.start()
        wsends.append(cp)

    def wsend_first():
        wsend(0, y, 0, yr, wrsem.at[0])
        wsend(1, y, 1, yl, wrsem.at[3])
        wsend(2, y, 1, yr, wrsem.at[1])
        wsend(3, y, 0, yl, wrsem.at[2])

    def wrelay():
        wait_bytes(wrows(yl, 0), wrsem.at[0])
        wsend(4, yl, 0, yr, wrsem.at[4])
        wait_bytes(wrows(yr, 1), wrsem.at[3])
        wsend(5, yr, 1, yl, wrsem.at[5])

    ysends = []

    def attended_send(n, src_of, tc, h):
        dst = abuf.at[h, c, :, :, pl.ds(pl.multiple_of(y * HD, HD), HD)]
        for dy in range(1, NY):
            yy = (y + dy) % NY
            cp = rcopy(src_of(yy), dst, ysend.at[n, dy], asem.at[h], dev(x, z, tc, yy))
            cp.start()
            ysends.append((cp, None))
        near = rcopy(src_of(y), dst, ysend.at[n, 0], asem.at[h], dev(x, z, oth, y))
        ysends.append((near, tc))

        @pl.when(c == tc)
        def _():
            pltpu.make_async_copy(src_of(y), dst, asem.at[h]).start()

        @pl.when(c != tc)
        def _():
            near.start()

    def quarter(ref):
        return lambda yy: ref.at[pl.ds(pl.multiple_of(yy * 16, 16), 16)]

    xr_, xl_, x2_ = (x + 1) % NX, (x + NX - 1) % NX, (x + 2) % NX

    def slot(xx, zz):
        return c * 64 + xx * NZ + zz

    def zm(d):
        return (z + d + NZ) % NZ

    def tsend_to(src, rs, to):
        rcopy(src, src, tsend, rs, to).start()

    def zcopies(step):
        for rel, dz, half in ZSENDS[step]:
            src = tiles.at[slot(x, zm(rel))]
            if half is not None:
                src = src.at[half]
            tsend_to(src, zsem.at[(rel - dz) % NZ if half != 1 else 0], dev(x, zm(dz), c, y))

    def zwait(group):
        for rel in ZGROUPS[group]:
            src = tiles.at[slot(x, zm(rel))]
            if rel == 8:
                wait_bytes(src.at[0], zsem.at[8])
                wait_bytes(src.at[1], zsem.at[0])
            else:
                wait_bytes(src, zsem.at[rel % NZ])

    def members(n):
        return [zm(rel) for rel in ZGROUPS[n]]

    partner = dev(x, z, oth, y)

    def forward(n):
        for zz in members(n):
            src = tiles.at[slot(x, zz)]
            tsend_to(src, xl.at[zz], dev(xr_, z, c, y))
            tsend_to(src, xr.at[zz], dev(xl_, z, c, y))
            tsend_to(src, psem, partner)
            if n == 4:
                tsend_to(src.at[0], x2sem.at[0], dev(x2_, z, c, y))
                tsend_to(src.at[1], x2sem.at[1], dev(x2_, z, c, y))

    def relay(n):
        for zz in members(n):
            src = tiles.at[slot(xl_, zz)]
            wait_bytes(src, xl.at[zz])
            if n < 4:
                tsend_to(src.at[0], x2sem.at[0], dev(xr_, z, c, y))
            tsend_to(src, psem, partner)
            src = tiles.at[slot(xr_, zz)]
            wait_bytes(src, xr.at[zz])
            if n < 4:
                tsend_to(src.at[1], x2sem.at[1], dev(xl_, z, c, y))
            tsend_to(src, psem, partner)

    src_id = x * NC + c

    def col_send(d):
        zz = zm(d)
        for dx in range(NX):
            g = (x + dx) % NX
            cp = rcopy(stage.at[zz * 4 + g], c2.at[src_id, z], a2s, a2r, dev(g, zz, OC, y))
            if d or dx:
                cp.start()
            else:

                @pl.when(c == OC)
                def _():
                    pltpu.make_async_copy(stage.at[zz * 4 + g], c2.at[src_id, z], a2r).start()

                @pl.when(c != OC)
                def _():
                    cp.start()

    wsend_first()
    for n in range(4):
        if n:
            zwait(n)
        zcopies(n)
        forward(n)
        if n == 0:
            pl.semaphore_wait(rowsem, NX * NC - 1)
        for d in SENDS[n]:
            col_send(d)
        if n >= 1:
            relay(n - 1)
        if n == 1:
            attended_send(0, quarter(orow), 0, 0)
        if n == 2:
            wrelay()
    zwait(4)
    forward(4)

    @pl.when(c == OC)
    def _():
        wait_bytes(c2, a2r)
        for t in range(3):
            cf[t] = c2[:, :, t].astype(F32).reshape(NBLK8, HD)

        def blk(r):
            return (r // 32) * 32 + (r % 16) * 2 + (r // 16) % 2

        rq = blk(lax.broadcasted_iota(jnp.int32, (128, 128), 0))
        rk = blk(lax.broadcasted_iota(jnp.int32, (128, 128), 1))
        ok = rq >= rk
        for j in range(8):
            cols = pl.ds(j, 128, stride=8)
            qc = cf[0, cols, :].astype(BF)
            kc = cf[1, cols, :].astype(BF)
            vc = cf[2, cols, :].astype(BF)
            s = jnp.where(ok, dot_t(qc, kc), NEG)
            m = jnp.max(s, axis=1, keepdims=True)
            p = jnp.exp2((s - m) * EXPC)
            l = jnp.sum(p, axis=1, keepdims=True)
            cfo[cols, :] = dot(p.astype(BF), vc) / l
        back = cfo[...].astype(BF).reshape(NX, NC, NZ, 8, HD)
        for cc in range(NC):
            obuf[:, :, cc] = back[:, cc]
        lanes = pl.ds(pl.multiple_of(y * HD, HD), HD)

        def give_back(i, carry):
            for zz in ((z + 8 - i) % NZ, (z + NZ - 7 + i) % NZ):
                for dx in range(NX):
                    xx = (x + dx) % NX
                    rcopy(
                        obuf.at[xx, zz],
                        abuf.at[1, :, (z % 4) * 4 + x, :, lanes],
                        r1s,
                        asem.at[1],
                        dev(xx, zz, 1, z // 4),
                    ).start()
            return carry

        lax.fori_loop(0, NZ // 2, give_back, 0)

    relay(3)
    relay(4)
    far2 = tiles.at[pl.ds(slot(x2_, 0), NZ)]
    wait_bytes(far2.at[:, 0], x2sem.at[0])
    wait_bytes(far2.at[:, 1], x2sem.at[1])
    tsend_to(far2, psem, partner)

    wait_bytes(tiles.at[pl.ds(oth * 64, 64)], psem)
    for f in range(2):
        for i in range(PICKS):
            t = lists[0, f, i]
            at = (t % 2) * 64 + t // 2
            fark[i * SUM : (i + 1) * SUM, :] = tiles[at, f, 0]
            farv[i * SUM : (i + 1) * SUM, :] = tiles[at, f, 1]
        for i in range(BLK // QC):
            rs = slice(i * QC, (i + 1) * QC)
            s = dot_t(q[rs, (2 + f) * HD : (3 + f) * HD], fark[...])
            s = jnp.where(jnp.full((QC, BLK), seq, jnp.int32) > 0, s, NEG)
            m0 = m_s[f, rs, :][:, :1]
            m = jnp.maximum(jnp.max(s, axis=1, keepdims=True), m0)
            p = jnp.exp2((s - m) * EXPC)
            shrink = jnp.exp2((m0 - m) * EXPC)
            l = l_s[f, rs, :][:, :1] * shrink + jnp.sum(p, axis=1, keepdims=True)
            acc = acc_s[f, rs, :] * shrink + dot(p.astype(BF), farv[...])
            ofix[f, i * (QC // 8) : (i + 1) * (QC // 8)] = (acc / l).astype(BF).reshape(QC // 8, 8, HD)
        attended_send(1 + f, quarter(ofix.at[f]), f, 1 - f)


    wait_bytes(wrows(yr, 0), wrsem.at[2])
    wait_bytes(wrows(y2, 0), wrsem.at[4])
    wait_bytes(abuf.at[0], asem.at[0])
    for i, at in enumerate((oth, c)):
        a = abuf[0, at].reshape(128, 512)
        for n in range(4):
            part[i, :, n * 512 : (n + 1) * 512] = dot(a, wbuf[:512, n * 512 : (n + 1) * 512])
    wait_bytes(wrows(yl, 1), wrsem.at[1])
    wait_bytes(wrows(y2, 1), wrsem.at[5])
    wait_bytes(abuf.at[1], asem.at[1])
    psends = []
    ap = abuf[1, oth].reshape(128, 512)
    for n in range(4):
        cols = slice(n * 512, (n + 1) * 512)
        pbuf[n] = (part[0, :, cols] + dot(ap, wbuf[512:, cols])).astype(BF)
        cp = rcopy(pbuf.at[n], prcv.at[n], fsend.at[n], frecv.at[n], partner)
        cp.start()
        psends.append(cp)
    ao = abuf[1, c].reshape(128, 512)
    for n in range(4):
        cols = slice(n * 512, (n + 1) * 512)
        po = part[1, :, cols] + dot(ao, wbuf[512:, cols])
        psends[n].wait_recv()
        out[:, cols] = (po + prcv[n].astype(F32)).astype(BF)

    for cp in psends:
        cp.wait_send()
    for cp in wsends:
        cp.wait_send()
    for cp, tc in ysends:
        if tc is None:
            cp.wait_send()
        else:
            @pl.when(c != tc)
            def _():
                cp.wait_send()
    wait_bytes(tiles.at[pl.ds(0, 127)], tsend)

    @pl.when(c != OC)
    def _():
        wait_bytes(stage, a2s)

    @pl.when(c == OC)
    def _():
        wait_bytes(stage.at[pl.ds(0, 63)], a2s)
        wait_bytes(obuf, r1s)


def hand_over(a, b):
    b[...] = a[...]


NBLK8 = NX * NZ * NC * 8


def per_device(queries, keys, values, summary_lists, out_weight):
    q3, k3, v3 = (a.reshape(64, 8, 512) for a in (queries, keys, values))
    vm = pl.BlockSpec(memory_space=pltpu.VMEM)
    anys = pl.BlockSpec(memory_space=pl.ANY)
    dma = pltpu.SemaphoreType.DMA
    mixed = pl.pallas_call(
        kernel,
        out_shape=jax.ShapeDtypeStruct((128, 2048), BF),
        in_specs=[anys] * 8,
        out_specs=vm,
        scratch_shapes=[
            pltpu.SMEM((1, 2, PICKS), jnp.int32),
            pltpu.VMEM((BLK, 512), BF),
            pltpu.VMEM((BLK, 512), BF),
            pltpu.VMEM((BLK, 512), BF),
            pltpu.VMEM((128, 2, 2, SUM, HD), BF),
            pltpu.VMEM((1024, 2048), BF),
            pltpu.VMEM((2, 2, 16, 8, 512), BF),
            pltpu.VMEM((2, 128, 2048), F32),
            pltpu.VMEM((64, 3, 8, HD), BF),
            pltpu.VMEM((NX * NC, NZ, 3, 8, HD), BF),
            pltpu.VMEM((NX, NZ, NC, 8, HD), BF),
            pltpu.VMEM((64, 8, HD), BF),
            pltpu.VMEM((2, 64, 8, HD), BF),
            pltpu.VMEM((3, NBLK8, HD), F32),
            pltpu.VMEM((NBLK8, HD), F32),
            pltpu.VMEM((2, BLK, HD), F32),
            pltpu.VMEM((2, BLK, HD), F32),
            pltpu.VMEM((2, BLK, HD), F32),
            pltpu.VMEM((BLK, HD), BF),
            pltpu.VMEM((BLK, HD), BF),
            pltpu.VMEM((4, 128, 512), BF),
            pltpu.VMEM((4, 128, 512), BF),
            dma((3,)), dma((9,)), dma((2,)), dma((6,)), dma((6,)), dma, dma((16,)), dma((16,)), dma((16,)), dma((2,)), dma,
            pltpu.SemaphoreType.REGULAR, dma, dma, dma, dma((3, 4)), dma((2,)), dma((4,)), dma((4,)),
        ],
        compiler_params=pltpu.CompilerParams(
            collective_id=0, has_side_effects=True, vmem_limit_bytes=67043328
        ),
    )(summary_lists, queries, keys, values, q3, k3, v3, out_weight)
    rows = pl.BlockSpec((64, 2048), lambda i: (i, 0))
    return pl.pallas_call(
        hand_over,
        grid=(2,),
        out_shape=jax.ShapeDtypeStruct((128, 2048), BF),
        in_specs=[rows],
        out_specs=rows,
        compiler_params=pltpu.CompilerParams(vmem_limit_bytes=67043328),
    )(mixed)


def solution(mesh):
    return jax.shard_map(
        per_device,
        mesh=mesh,
        in_specs=(
            P("seq", "head"),
            P("seq", "head"),
            P("seq", "head"),
            P("seq", "head", None),
            P("head", None),
        ),
        out_specs=P(("seq", "head"), None),
        check_vma=False,
    )
```

```python
import functools
import math

import jax
import jax.numpy as jnp
from jax import lax
from jax.experimental import pallas as pl
from jax.experimental.pallas import tpu as pltpu
from jax.sharding import PartitionSpec as P

MESH = pl.DeviceIdType.MESH
HD = 128
BLK = 512
NX, NZ, NC, NY = 4, 16, 2, 4
PICKS = 16
SUM = 32
NEG = -1e30
EXPC = (HD ** -0.5) * math.log2(math.e)
QC = 256
OC = 0
ZGROUPS = ((0,), (-5, 5, -1, 1), (-6, 6, -4, 4, -2, 2), (-7, 7, -3, 3), (8,))
ZSENDS = (
    ((0, 5, None), (0, -5, None), (0, 1, None), (0, -1, None)),
    ((-5, 1, None), (5, -1, None), (-5, -1, None), (5, 1, None), (-1, 1, None), (1, -1, None)),
    ((-6, 1, None), (6, -1, None), (-4, -1, None), (4, 1, None)),
    ((-7, 1, 0), (7, -1, 1)),
)
SENDS = ((8, 7, -7, 0, 1, -1), (6, -6, 5, -5, 4, -4), (3, -3, 2, -2), ())
BF = jnp.bfloat16
F32 = jnp.float32


def dot_t(a, b):
    return lax.dot_general(a, b, (((1,), (1,)), ((), ())), preferred_element_type=F32)


def dot(a, b):
    return jnp.dot(a, b, preferred_element_type=F32)


def kernel(
    lists_h, q_h, k_h, v_h, q3, k3, v3, w,
    out,
    lists, q, k, v,
    tiles, wbuf, abuf, part, stage, c2, obuf, orow, ofix,
    cf, cfo, acc_s, m_s, l_s, fark, farv, pbuf, prcv,
    qsem, lsem, wlsem, wssem, wrsem, tsend, zsem, xl, xr, x2sem, psem,
    rowsem, a2s, a2r, r1s, ysend, asem, fsend, frecv,
):
    seq = lax.axis_index("seq")
    y = lax.axis_index("head")
    x = seq // (NZ * NC)
    z = (seq // NC) % NZ
    c = seq % NC
    oth = 1 - c

    def dev(xx, zz, cc, yy):
        return ((xx * NZ + zz) * NC + cc, yy)

    def rcopy(src, dst, ss, rs, to):
        return pltpu.make_async_remote_copy(
            src_ref=src, dst_ref=dst, send_sem=ss, recv_sem=rs, device_id=to, device_id_type=MESH
        )

    def wait_bytes(ref, sem):
        pltpu.make_async_copy(ref, ref, sem).wait()

    loads = []
    for t, (src, dst) in enumerate(((q_h, q), (k_h, k), (v_h, v))):
        loads.append(pltpu.make_async_copy(src, dst, qsem.at[t]))
        loads[-1].start()

    bar = pltpu.get_barrier_semaphore()

    def greet(to):
        pl.semaphore_signal(bar, inc=1, device_id=to, device_id_type=MESH)

    def greet_z(i, carry):
        greet(dev(x, (z + i) % NZ, c, y))
        return carry

    lax.fori_loop(1, NZ, greet_z, 0)
    for dx in range(NX):
        for dc in range(NC):
            if dx or dc:
                greet(dev((x + dx) % NX, z, (c + dc) % NC, y))
    for dy in range(1, NY):
        for dc in range(NC):
            greet(dev(x, z, (c + dc) % NC, (y + dy) % NY))

    own = c * 64 + x * NZ + z
    local = []
    for t, src in enumerate((q3, k3, v3)):
        local.append(pltpu.make_async_copy(src.at[:, :, HD : 2 * HD], stage.at[:, t], lsem.at[t]))
    local.append(pltpu.make_async_copy(lists_h, lists, lsem.at[8]))
    for f in range(2):
        for t, src in enumerate((k_h, v_h)):
            local.append(
                pltpu.make_async_copy(
                    src.at[BLK - SUM : BLK, (2 + f) * HD : (3 + f) * HD],
                    tiles.at[own, f, t],
                    lsem.at[3 + 2 * f + t],
                )
            )
    for h in range(2):
        local.append(
            pltpu.make_async_copy(
                w.at[pl.ds(pl.multiple_of((2 - c if h else 3 * c) * HD, HD), HD)],
                wbuf.at[pl.ds(pl.multiple_of((h * NY + y) * HD, HD), HD)],
                wlsem.at[h],
            )
        )
    for cp in local:
        cp.start()

    def own_attention(head, i):
        qi = q[i * QC : (i + 1) * QC, head * HD : (head + 1) * HD]
        n = (i + 1) * QC
        s = dot_t(qi, k[:n, head * HD : (head + 1) * HD])
        rows = lax.broadcasted_iota(jnp.int32, (QC, n), 0) + i * QC
        cols = lax.broadcasted_iota(jnp.int32, (QC, n), 1)
        s = jnp.where(rows >= cols, s, NEG)
        m = jnp.max(s, axis=1, keepdims=True)
        p = jnp.exp2((s - m) * EXPC)
        l = jnp.sum(p, axis=1, keepdims=True)
        acc = dot(p.astype(BF), v[:n, head * HD : (head + 1) * HD])
        return m, l, acc

    for cp in loads:
        cp.wait()
    for i in range(BLK // QC):
        m, l, acc = own_attention(0, i)
        orow[i * (QC // 8) : (i + 1) * (QC // 8)] = (acc / l).astype(BF).reshape(QC // 8, 8, HD)
    for f in range(2):
        for i in range(BLK // QC):
            m, l, acc = own_attention(2 + f, i)
            rs = slice(i * QC, (i + 1) * QC)
            acc_s[f, rs, :] = acc
            m_s[f, rs, :] = jnp.broadcast_to(m, (QC, HD))
            l_s[f, rs, :] = jnp.broadcast_to(l, (QC, HD))

    for cp in local:
        cp.wait()
    pl.semaphore_wait(bar, (NZ - 1) + (NX * NC - 1) + (NY - 1) * NC)
    for dx in range(NX):
        for dc in range(NC):
            if dx or dc:
                pl.semaphore_signal(
                    rowsem, inc=1, device_id=dev((x + dx) % NX, z, (c + dc) % NC, y), device_id_type=MESH
                )

    def wrows(yy, h):
        return wbuf.at[pl.ds(pl.multiple_of((h * NY + yy) * HD, HD), HD)]

    yr, yl, y2 = (y + 1) % NY, (y + NY - 1) % NY, (y + 2) % NY
    wsends = []

    def wsend(n, yy, h, to, rsem):
        cp = rcopy(wrows(yy, h), wrows(yy, h), wssem.at[n], rsem, dev(x, z, c, to))
        cp.start()
        wsends.append(cp)

    def wsend_first():
        wsend(0, y, 0, yr, wrsem.at[0])
        wsend(1, y, 1, yl, wrsem.at[3])
        wsend(2, y, 1, yr, wrsem.at[1])
        wsend(3, y, 0, yl, wrsem.at[2])

    def wrelay():
        wait_bytes(wrows(yl, 0), wrsem.at[0])
        wsend(4, yl, 0, yr, wrsem.at[4])
        wait_bytes(wrows(yr, 1), wrsem.at[3])
        wsend(5, yr, 1, yl, wrsem.at[5])

    ysends = []

    def attended_send(n, src_of, tc, h):
        dst = abuf.at[h, c, :, :, pl.ds(pl.multiple_of(y * HD, HD), HD)]
        for dy in range(1, NY):
            yy = (y + dy) % NY
            cp = rcopy(src_of(yy), dst, ysend.at[n, dy], asem.at[h], dev(x, z, tc, yy))
            cp.start()
            ysends.append((cp, None))
        near = rcopy(src_of(y), dst, ysend.at[n, 0], asem.at[h], dev(x, z, oth, y))
        ysends.append((near, tc))

        @pl.when(c == tc)
        def _():
            pltpu.make_async_copy(src_of(y), dst, asem.at[h]).start()

        @pl.when(c != tc)
        def _():
            near.start()

    def quarter(ref):
        return lambda yy: ref.at[pl.ds(pl.multiple_of(yy * 16, 16), 16)]

    xr_, xl_, x2_ = (x + 1) % NX, (x + NX - 1) % NX, (x + 2) % NX

    def slot(xx, zz):
        return c * 64 + xx * NZ + zz

    def zm(d):
        return (z + d + NZ) % NZ

    def tsend_to(src, rs, to):
        rcopy(src, src, tsend, rs, to).start()

    def zcopies(step):
        for rel, dz, half in ZSENDS[step]:
            src = tiles.at[slot(x, zm(rel))]
            if half is not None:
                src = src.at[half]
            tsend_to(src, zsem.at[(rel - dz) % NZ if half != 1 else 0], dev(x, zm(dz), c, y))

    def zwait(group):
        for rel in ZGROUPS[group]:
            src = tiles.at[slot(x, zm(rel))]
            if rel == 8:
                wait_bytes(src.at[0], zsem.at[8])
                wait_bytes(src.at[1], zsem.at[0])
            else:
                wait_bytes(src, zsem.at[rel % NZ])

    def members(n):
        return [zm(rel) for rel in ZGROUPS[n]]

    partner = dev(x, z, oth, y)

    def forward(n):
        for zz in members(n):
            src = tiles.at[slot(x, zz)]
            tsend_to(src, xl.at[zz], dev(xr_, z, c, y))
            tsend_to(src, xr.at[zz], dev(xl_, z, c, y))
            tsend_to(src, psem, partner)
            if n == 4:
                tsend_to(src.at[0], x2sem.at[0], dev(x2_, z, c, y))
                tsend_to(src.at[1], x2sem.at[1], dev(x2_, z, c, y))

    def relay(n):
        for zz in members(n):
            src = tiles.at[slot(xl_, zz)]
            wait_bytes(src, xl.at[zz])
            if n < 4:
                tsend_to(src.at[0], x2sem.at[0], dev(xr_, z, c, y))
            tsend_to(src, psem, partner)
            src = tiles.at[slot(xr_, zz)]
            wait_bytes(src, xr.at[zz])
            if n < 4:
                tsend_to(src.at[1], x2sem.at[1], dev(xl_, z, c, y))
            tsend_to(src, psem, partner)

    src_id = x * NC + c

    def col_send(d):
        zz = zm(d)
        for dx in range(NX):
            g = (x + dx) % NX
            cp = rcopy(stage.at[zz * 4 + g], c2.at[src_id, z], a2s, a2r, dev(g, zz, OC, y))
            if d or dx:
                cp.start()
            else:

                @pl.when(c == OC)
                def _():
                    pltpu.make_async_copy(stage.at[zz * 4 + g], c2.at[src_id, z], a2r).start()

                @pl.when(c != OC)
                def _():
                    cp.start()

    wsend_first()
    for n in range(4):
        if n:
            zwait(n)
        zcopies(n)
        forward(n)
        if n == 0:
            pl.semaphore_wait(rowsem, NX * NC - 1)
        for d in SENDS[n]:
            col_send(d)
        if n >= 1:
            relay(n - 1)
        if n == 1:
            attended_send(0, quarter(orow), 0, 0)
        if n == 2:
            wrelay()
    zwait(4)
    forward(4)

    @pl.when(c == OC)
    def _():
        wait_bytes(c2, a2r)
        for t in range(3):
            cf[t] = c2[:, :, t].astype(F32).reshape(NBLK8, HD)

        def blk(r):
            return (r // 32) * 32 + (r % 16) * 2 + (r // 16) % 2

        rq = blk(lax.broadcasted_iota(jnp.int32, (128, 128), 0))
        rk = blk(lax.broadcasted_iota(jnp.int32, (128, 128), 1))
        ok = rq >= rk
        for j in range(8):
            cols = pl.ds(j, 128, stride=8)
            qc = cf[0, cols, :].astype(BF)
            kc = cf[1, cols, :].astype(BF)
            vc = cf[2, cols, :].astype(BF)
            s = jnp.where(ok, dot_t(qc, kc), NEG)
            m = jnp.max(s, axis=1, keepdims=True)
            p = jnp.exp2((s - m) * EXPC)
            l = jnp.sum(p, axis=1, keepdims=True)
            cfo[cols, :] = dot(p.astype(BF), vc) / l
        back = cfo[...].astype(BF).reshape(NX, NC, NZ, 8, HD)
        for cc in range(NC):
            obuf[:, :, cc] = back[:, cc]
        lanes = pl.ds(pl.multiple_of(y * HD, HD), HD)

        def give_back(i, carry):
            for zz in ((z + 8 - i) % NZ, (z + NZ - 7 + i) % NZ):
                for dx in range(NX):
                    xx = (x + dx) % NX
                    rcopy(
                        obuf.at[xx, zz],
                        abuf.at[1, :, (z % 4) * 4 + x, :, lanes],
                        r1s,
                        asem.at[1],
                        dev(xx, zz, 1, z // 4),
                    ).start()
            return carry

        lax.fori_loop(0, NZ // 2, give_back, 0)

    relay(3)
    relay(4)
    far2 = tiles.at[pl.ds(slot(x2_, 0), NZ)]
    wait_bytes(far2.at[:, 0], x2sem.at[0])
    wait_bytes(far2.at[:, 1], x2sem.at[1])
    tsend_to(far2, psem, partner)

    wait_bytes(tiles.at[pl.ds(oth * 64, 64)], psem)
    for f in range(2):
        for i in range(PICKS):
            t = lists[0, f, i]
            at = (t % 2) * 64 + t // 2
            fark[i * SUM : (i + 1) * SUM, :] = tiles[at, f, 0]
            farv[i * SUM : (i + 1) * SUM, :] = tiles[at, f, 1]
        for i in range(BLK // QC):
            rs = slice(i * QC, (i + 1) * QC)
            s = dot_t(q[rs, (2 + f) * HD : (3 + f) * HD], fark[...])
            s = jnp.where(jnp.full((QC, BLK), seq, jnp.int32) > 0, s, NEG)
            m0 = m_s[f, rs, :][:, :1]
            m = jnp.maximum(jnp.max(s, axis=1, keepdims=True), m0)
            p = jnp.exp2((s - m) * EXPC)
            shrink = jnp.exp2((m0 - m) * EXPC)
            l = l_s[f, rs, :][:, :1] * shrink + jnp.sum(p, axis=1, keepdims=True)
            acc = acc_s[f, rs, :] * shrink + dot(p.astype(BF), farv[...])
            ofix[f, i * (QC // 8) : (i + 1) * (QC // 8)] = (acc / l).astype(BF).reshape(QC // 8, 8, HD)
        attended_send(1 + f, quarter(ofix.at[f]), f, 1 - f)


    wait_bytes(wrows(yr, 0), wrsem.at[2])
    wait_bytes(wrows(y2, 0), wrsem.at[4])
    wait_bytes(abuf.at[0], asem.at[0])
    for i, at in enumerate((oth, c)):
        a = abuf[0, at].reshape(128, 512)
        for n in range(4):
            part[i, :, n * 512 : (n + 1) * 512] = dot(a, wbuf[:512, n * 512 : (n + 1) * 512])
    wait_bytes(wrows(yl, 1), wrsem.at[1])
    wait_bytes(wrows(y2, 1), wrsem.at[5])
    wait_bytes(abuf.at[1], asem.at[1])
    psends = []
    ap = abuf[1, oth].reshape(128, 512)
    for n in range(4):
        cols = slice(n * 512, (n + 1) * 512)
        pbuf[n] = (part[0, :, cols] + dot(ap, wbuf[512:, cols])).astype(BF)
        cp = rcopy(pbuf.at[n], prcv.at[n], fsend.at[n], frecv.at[n], partner)
        cp.start()
        psends.append(cp)
    ao = abuf[1, c].reshape(128, 512)
    for n in range(4):
        cols = slice(n * 512, (n + 1) * 512)
        po = part[1, :, cols] + dot(ao, wbuf[512:, cols])
        psends[n].wait_recv()
        out[:, cols] = (po + prcv[n].astype(F32)).astype(BF)

    for cp in psends:
        cp.wait_send()
    for cp in wsends:
        cp.wait_send()
    for cp, tc in ysends:
        if tc is None:
            cp.wait_send()
        else:
            @pl.when(c != tc)
            def _():
                cp.wait_send()
    wait_bytes(tiles.at[pl.ds(0, 127)], tsend)

    @pl.when(c != OC)
    def _():
        wait_bytes(stage, a2s)

    @pl.when(c == OC)
    def _():
        wait_bytes(stage.at[pl.ds(0, 63)], a2s)
        wait_bytes(obuf, r1s)


def hand_over(a, b):
    b[...] = a[...]


NBLK8 = NX * NZ * NC * 8


def per_device(queries, keys, values, summary_lists, out_weight):
    q3, k3, v3 = (a.reshape(64, 8, 512) for a in (queries, keys, values))
    vm = pl.BlockSpec(memory_space=pltpu.VMEM)
    anys = pl.BlockSpec(memory_space=pl.ANY)
    dma = pltpu.SemaphoreType.DMA
    mixed = pl.pallas_call(
        kernel,
        out_shape=jax.ShapeDtypeStruct((128, 2048), BF),
        in_specs=[anys] * 8,
        out_specs=vm,
        scratch_shapes=[
            pltpu.SMEM((1, 2, PICKS), jnp.int32),
            pltpu.VMEM((BLK, 512), BF),
            pltpu.VMEM((BLK, 512), BF),
            pltpu.VMEM((BLK, 512), BF),
            pltpu.VMEM((128, 2, 2, SUM, HD), BF),
            pltpu.VMEM((1024, 2048), BF),
            pltpu.VMEM((2, 2, 16, 8, 512), BF),
            pltpu.VMEM((2, 128, 2048), F32),
            pltpu.VMEM((64, 3, 8, HD), BF),
            pltpu.VMEM((NX * NC, NZ, 3, 8, HD), BF),
            pltpu.VMEM((NX, NZ, NC, 8, HD), BF),
            pltpu.VMEM((64, 8, HD), BF),
            pltpu.VMEM((2, 64, 8, HD), BF),
            pltpu.VMEM((3, NBLK8, HD), F32),
            pltpu.VMEM((NBLK8, HD), F32),
            pltpu.VMEM((2, BLK, HD), F32),
            pltpu.VMEM((2, BLK, HD), F32),
            pltpu.VMEM((2, BLK, HD), F32),
            pltpu.VMEM((BLK, HD), BF),
            pltpu.VMEM((BLK, HD), BF),
            pltpu.VMEM((4, 128, 512), BF),
            pltpu.VMEM((4, 128, 512), BF),
            dma((3,)), dma((9,)), dma((2,)), dma((6,)), dma((6,)), dma, dma((16,)), dma((16,)), dma((16,)), dma((2,)), dma,
            pltpu.SemaphoreType.REGULAR, dma, dma, dma, dma((3, 4)), dma((2,)), dma((4,)), dma((4,)),
        ],
        compiler_params=pltpu.CompilerParams(
            collective_id=0, has_side_effects=True, vmem_limit_bytes=67043328
        ),
    )(summary_lists, queries, keys, values, q3, k3, v3, out_weight)
    rows = pl.BlockSpec((64, 2048), lambda i: (i, 0))
    return pl.pallas_call(
        hand_over,
        grid=(2,),
        out_shape=jax.ShapeDtypeStruct((128, 2048), BF),
        in_specs=[rows],
        out_specs=rows,
        compiler_params=pltpu.CompilerParams(vmem_limit_bytes=67043328),
    )(mixed)


def solution(mesh):
    return jax.shard_map(
        per_device,
        mesh=mesh,
        in_specs=(
            P("seq", "head"),
            P("seq", "head"),
            P("seq", "head"),
            P("seq", "head", None),
            P("head", None),
        ),
        out_specs=P(("seq", "head"), None),
        check_vma=False,
    )
```
